32 devices in a mesh: seq: 8 (over z, x), dp: 4 (over y, core).
Axes of the slice: x: 2, y: 2, z: 4, core: 2. Of those that a mesh axis runs over, the one named last changes fastest.
Arguments:
- layer_input: bfloat16 [4, 1024, 4096], P('dp', 'seq'), may hold values from -6 to 6
- projection: bfloat16 [4096, 256], replicated, may hold values from -0.09375 to 0.09375
- ssm_input: bfloat16 [4, 1024, 4096], P('dp', 'seq'), may hold values from -6 to 6
- step_logit: float32 [4, 1024, 64], P('dp', 'seq'), may hold values from -4 to 4
- decay_rate: float32 [64], replicated, may hold values from 0.00048828125 to 0.1
- output_grad: bfloat16 [4, 1024, 4096], P('dp', 'seq'), may hold values from -6 to 6
Outputs:
- input_grad: bfloat16 [4, 1024, 4096], P('dp', 'seq')
- step_grad: float32 [4, 1024, 64], P('dp', 'seq')
- rate_grad: float32 [64], replicated
- projection_grad: float32 [4096, 256], P('seq')
The draws below stay inside these ranges and needn't reach their ends.
All inputs are finite; a program needn't handle non-finite values.
Results may differ from the reference program's by a relative error of at most 0.011.
Values sent between devices are 32-bit elements; how exact they have to be, the bound alone decides.
A program may use at most 320 MiB of HBM per device.

```python
import math
import jax
import jax.numpy as jnp
from jax import lax

D = 4096
H = 64
P_SIZE = 64
N = 128
L_DEV = 128
HP = 4096
LENGTH = 1024
TRACES = 4


def shard_levels(stream_key, dims, split, smallest, high):
    level = 1.0
    for position, parts in split:
        heights = jax.random.uniform(jax.random.fold_in(jax.random.fold_in(stream_key, 6), position), (parts,), jnp.float32, smallest / len(split), high / len(split))
        level = level * jnp.repeat(jnp.exp(heights), dims[position] // parts).reshape((-1,) + (1,) * (len(dims) - 1 - position))
    return level


def bell_draw(own_key, shape, width, most, cuts=(), dtype=jnp.bfloat16):
    values = jax.random.normal(own_key, shape, jnp.float32) * width
    if len(cuts) > 0:
        values = shard_levels(own_key, shape, cuts, -0.22, 0.18) * values
    return jnp.clip(values, min=-most, max=most).astype(dtype)


def setup_inputs(seed: int = 0) -> dict:
    key_list = jax.random.split(jax.random.key(seed), 7)
    return {
        "layer_input": bell_draw(key_list[0], (TRACES, LENGTH, D), 1.0, 6.0, ((0, 4), (1, 8))),
        "projection": bell_draw(key_list[1], (D, 2 * N), D ** -0.5, 0.09375),
        "ssm_input": bell_draw(key_list[2], (TRACES, LENGTH, HP), 1.0, 6.0, ((0, 4), (1, 8))),
        "step_logit": bell_draw(key_list[3], (TRACES, LENGTH, H), 1.0, 4.0, ((0, 4), (1, 8)), jnp.float32),
        "decay_rate": jnp.clip(jnp.exp(jax.random.uniform(key_list[4], (H,), jnp.float32, math.log(0.00048828125), math.log(0.1))), 0.00048828125, 0.1),
        "output_grad": bell_draw(key_list[5], (TRACES, LENGTH, HP), 1.0, 6.0, ((0, 4), (1, 8))),
    }


def span_forward(ssm_block, b_block, c_block, logit_block, decay_rate, carry_in):
    row_count = ssm_block.shape[0]
    head_count = logit_block.shape[1]
    values = ssm_block.astype(jnp.float32).reshape(row_count, head_count, -1)
    b_vals = b_block.astype(jnp.float32)
    c_vals = c_block.astype(jnp.float32)
    dt_soft = jax.nn.softplus(logit_block)
    log_decay = jnp.cumsum(-decay_rate[None, :] * dt_soft, axis=0)
    causal = (lax.broadcasted_iota(jnp.int32, (row_count, row_count), 0) >= lax.broadcasted_iota(jnp.int32, (row_count, row_count), 1))[None, :, :]
    decay_heads = log_decay.T
    gap_log = decay_heads[:, :, None] - decay_heads[:, None, :]
    decays = jnp.exp(jnp.where(causal, gap_log, -jnp.inf))
    scores = jnp.einsum('tn,sn->ts', c_vals, b_vals, precision=lax.Precision.HIGHEST)
    weights = decays * scores[None, :, :] * dt_soft.T[:, None, :]
    inner = jnp.einsum('hts,shp->thp', weights, values, precision=lax.Precision.HIGHEST)
    outer = jnp.exp(log_decay)[:, :, None] * jnp.einsum('tn,hpn->thp', c_vals, carry_in, precision=lax.Precision.HIGHEST)
    to_end = jnp.exp(log_decay[-1][None, :] - log_decay) * dt_soft
    carry_out = jnp.exp(log_decay[-1])[:, None, None] * carry_in + jnp.einsum('sh,shp,sn->hpn', to_end, values, b_vals, precision=lax.Precision.HIGHEST)
    return (inner + outer, carry_out)

def reference(layer_input, projection, ssm_input, step_logit, decay_rate, output_grad):
    state_size = projection.shape[1] // 2

    def one_trace(items):
        tokens, x_rows, logit_rows, grad_rows = items
        projected = jnp.dot(tokens, projection, preferred_element_type=jnp.float32).astype(jnp.bfloat16)

        def forward(x_all, b_all, c_all, logit_all, rate_vec):
            blocks = (x_all.reshape(-1, L_DEV, x_all.shape[1]), b_all.reshape(-1, L_DEV, state_size), c_all.reshape(-1, L_DEV, state_size), logit_all.reshape(-1, L_DEV, logit_all.shape[1]))

            def advance(carry, block):
                result, carry_next = span_forward(block[0], block[1], block[2], block[3], rate_vec, carry)
                return (carry_next, result)
            start = jnp.zeros((H, P_SIZE, state_size), jnp.float32)
            unused, outputs = lax.scan(jax.checkpoint(advance), start, blocks)
            return outputs
        unused, pullback = jax.vjp(forward, x_rows, projected[:, :state_size], projected[:, state_size:], logit_rows, decay_rate)
        grad_x, grad_b, grad_c, grad_logit, grad_rate = pullback(grad_rows.astype(jnp.float32).reshape(-1, L_DEV, H, P_SIZE))
        grad_bc = jnp.concatenate([grad_b, grad_c], axis=1)
        grad_w = lax.dot_general(tokens, grad_bc, (((0,), (0,)), ((), ())), preferred_element_type=jnp.float32)
        return (grad_x, grad_logit, grad_rate, grad_w)
    grad_x, grad_logit, grad_rate, grad_w = lax.map(one_trace, (layer_input, ssm_input, step_logit, output_grad))
    return (grad_x, grad_logit, lax.optimization_barrier(jnp.sum(grad_rate, axis=0)), lax.optimization_barrier(jnp.sum(grad_w, axis=0)))
```

```python
import functools

import jax
import jax.numpy as jnp
from jax import lax
from jax.experimental import pallas as pl
from jax.experimental.pallas import tpu as pltpu
from jax.sharding import PartitionSpec as P

F32 = jnp.float32
BF16 = jnp.bfloat16
HEADS = 8


def dot(a, b, ca, cb):
    return lax.dot_general(a, b, (((ca,), (cb,)), ((), ())), preferred_element_type=F32)


def pair_columns(cols, j, size):
    rows = cols.shape[0]
    lane = lax.broadcasted_iota(jnp.int32, (rows, 2 * size), 1)
    return jnp.where(lane < size, cols[:, j : j + 1], cols[:, j + 1 : j + 2])


def local_kernel(size, b_ref, c_ref, x_ref, g_ref, col_ref, s_ref, a_ref):
    cols = col_ref[0]
    width = 2 * size
    for pair in range(HEADS // 2):
        lanes = pl.ds(pair * width, width)
        j = 2 * pair
        to_end = pair_columns(cols, j + HEADS, size) * pair_columns(cols, j + 2 * HEADS, size)
        grow = pair_columns(cols, j + 3 * HEADS, size)
        xs = (x_ref[:, lanes].astype(F32) * to_end).astype(BF16)
        gs = (g_ref[:, lanes].astype(F32) * grow).astype(BF16)
        s_ref[0, :, lanes] = dot(b_ref[...], xs, 0, 0)
        a_ref[0, :, lanes] = dot(c_ref[...], gs, 0, 0)


def scan_kernel(
    n, d_ref, s_ref, a_ref, e_out, f_out,
    d_in, s_in, a_in, e_in, f_in, e_snd, f_snd,
    d_sem, s_sem, a_sem, e_sem, f_sem,
):
    chunks = s_ref.shape[0]
    nz = n // 2
    me = lax.axis_index("seq")
    odd = lax.rem(me, 2)
    z = lax.div(me, 2)
    partner = me + 1 - 2 * odd
    first, last = z == 0, z == nz - 1
    barrier = pltpu.get_barrier_semaphore()

    def greet(who):
        pl.semaphore_signal(
            barrier, inc=1, device_id={"seq": who}, device_id_type=pl.DeviceIdType.MESH
        )

    greet(partner)
    pl.when(jnp.logical_not(first))(lambda: greet(me - 2))
    pl.when(jnp.logical_not(last))(lambda: greet(me + 2))
    end = jnp.logical_or(first, last)
    pl.when(end)(lambda: pl.semaphore_wait(barrier, min(nz, 2)))
    pl.when(jnp.logical_not(end))(lambda: pl.semaphore_wait(barrier, 3))

    def send(src, dst, sems, k, who):
        return pltpu.make_async_remote_copy(
            src_ref=src, dst_ref=dst, send_sem=sems.at[0, k], recv_sem=sems.at[1, k],
            device_id={"seq": who}, device_id_type=pl.DeviceIdType.MESH,
        )

    def copy_d():
        return send(d_ref, d_in, d_sem, 0, partner)

    def copy_s(k):
        return send(s_ref.at[k], s_in.at[k], s_sem, k, partner)

    def copy_a(k):
        return send(a_ref.at[k], a_in.at[k], a_sem, k, partner)

    def copy_e(k):
        return send(e_snd.at[k], e_in.at[k], e_sem, k, me + 2)

    def copy_f(k):
        return send(f_snd.at[k], f_in.at[k], f_sem, k, me - 2)

    copy_d().start()
    for k in range(chunks):
        copy_s(k).start()
        copy_a(k).start()

    @pl.when(first)
    def _():
        e_in[...] = jnp.zeros_like(e_in)

    @pl.when(last)
    def _():
        f_in[...] = jnp.zeros_like(f_in)

    copy_d().wait_recv()

    def advance(k, near, far, carry, out, snd, near_first):
        @pl.when(near_first)
        def _():
            value = carry[k]
            out[k] = value.astype(out.dtype)
            middle = d_ref[k, 0:1] * value + near[k]
            snd[k] = d_in[k, 0:1] * middle + far[k]

        @pl.when(jnp.logical_not(near_first))
        def _():
            middle = d_in[k, 0:1] * carry[k] + far[k]
            out[k] = middle.astype(out.dtype)
            snd[k] = d_ref[k, 0:1] * middle + near[k]

    def step(t, unused):
        kf = t - z

        @pl.when(jnp.logical_and(kf >= 0, kf < chunks))
        def _():
            copy_s(kf).wait_recv()
            pl.when(jnp.logical_not(first))(lambda: copy_e(kf).wait_recv())
            advance(kf, s_ref, s_in, e_in, e_out, e_snd, odd == 0)
            pl.when(jnp.logical_not(last))(lambda: copy_e(kf).start())

        kb = t - (nz - 1 - z)

        @pl.when(jnp.logical_and(kb >= 0, kb < chunks))
        def _():
            copy_a(kb).wait_recv()
            pl.when(jnp.logical_not(last))(lambda: copy_f(kb).wait_recv())
            advance(kb, a_ref, a_in, f_in, f_out, f_snd, odd == 1)
            pl.when(jnp.logical_not(first))(lambda: copy_f(kb).start())

        return unused

    lax.fori_loop(0, chunks + nz - 1, step, 0)
    copy_d().wait_send()
    for k in range(chunks):
        copy_s(k).wait_send()
        copy_a(k).wait_send()

    @pl.when(jnp.logical_not(last))
    def _():
        for k in range(chunks):
            copy_e(k).wait_send()

    @pl.when(jnp.logical_not(first))
    def _():
        for k in range(chunks):
            copy_f(k).wait_send()


def grad_kernel(
    size, b_ref, c_ref, x_ref, g_ref, col_ref, row_ref, e_ref, f_ref,
    dx_ref, rows_ref, cols_ref, ef_ref, gbc_ref,
    scores, d_scores, d_b, d_c,
):
    group = pl.program_id(0)
    b, c = b_ref[...], c_ref[...]
    length = b.shape[0]
    width = 2 * size

    @pl.when(group == 0)
    def _():
        scores[...] = dot(b, c, 1, 1)
        d_scores[...] = jnp.zeros_like(d_scores)
        d_b[...] = jnp.zeros_like(d_b)
        d_c[...] = jnp.zeros_like(d_c)

    cols = col_ref[0]
    rows = row_ref[...]
    k_st = scores[...]
    causal = lax.broadcasted_iota(jnp.int32, (length, length), 1) >= lax.broadcasted_iota(
        jnp.int32, (length, length), 0
    )
    lane = lax.broadcasted_iota(jnp.int32, (length, width), 1)
    low = lane < size
    place = lax.broadcasted_iota(jnp.int32, (length, cols_ref.shape[2]), 1)
    result = jnp.zeros((length, cols_ref.shape[2]), F32)
    q_sum = d_scores[...]
    b_sum, c_sum = d_b[...], d_c[...]
    for pair in range(HEADS // 2):
        lanes = pl.ds(pair * width, width)
        x2, g2 = x_ref[:, lanes], g_ref[:, lanes]
        x2f, g2f = x2.astype(F32), g2.astype(F32)
        e2, f2 = e_ref[0, :, lanes], f_ref[0, :, lanes]
        j = 2 * pair
        dt2 = pair_columns(cols, j + HEADS, size)
        end2 = pair_columns(cols, j + 2 * HEADS, size)
        grow2 = pair_columns(cols, j + 3 * HEADS, size)
        g_low = jnp.where(low, g2, jnp.zeros_like(g2))
        g_high = jnp.where(low, jnp.zeros_like(g2), g2)
        g_both = jnp.concatenate([g_low, g_high], axis=0)
        gram = dot(x2, g_both, 1, 1)
        weights = []
        for side in range(2):
            h = j + side
            gap = rows[h : h + 1, :] - cols[:, h : h + 1]
            decay = jnp.exp(jnp.where(causal, gap, -jnp.inf))
            mg = decay * gram[:, side * length : (side + 1) * length]
            dt = cols[:, h + HEADS : h + HEADS + 1]
            q_sum = q_sum + mg * dt
            raw = mg * k_st
            rows_ref[h : h + 1, :] = jnp.sum(raw * dt, axis=0, keepdims=True)
            result = jnp.where(place == h, jnp.sum(raw, axis=1, keepdims=True), result)
            weights.append((decay * k_st).astype(BF16))
        z2 = dot(jnp.concatenate(weights, axis=1), g_both, 1, 0)
        z_in = dot(b, f2, 1, 0) * end2
        dx_ref[:, lanes] = (dt2 * (z2 + z_in)).astype(dx_ref.dtype)
        y_in = dot(c, e2, 1, 0) * grow2
        xz, gy = x2f * z_in, g2f * y_in
        zero = jnp.zeros_like(xz)
        for side in range(2):
            h = j + side
            mask = low if side == 0 else jnp.logical_not(low)
            xs = jnp.sum(jnp.where(mask, xz, zero), axis=1, keepdims=True)
            gs = jnp.sum(jnp.where(mask, gy, zero), axis=1, keepdims=True)
            result = jnp.where(place == h + HEADS, xs, result)
            result = jnp.where(place == h + 2 * HEADS, gs, result)
        ef_ref[0, :, lanes] = jnp.sum(e2.astype(F32) * f2.astype(F32), axis=0, keepdims=True)
        b_sum = b_sum + dot((x2f * (end2 * dt2)).astype(BF16), f2, 1, 1)
        c_sum = c_sum + dot((g2f * grow2).astype(BF16), e2, 1, 1)
    cols_ref[0] = result
    d_scores[...] = q_sum
    d_b[...] = b_sum
    d_c[...] = c_sum

    @pl.when(group == pl.num_programs(0) - 1)
    def _():
        dk = q_sum.astype(BF16)
        state = b.shape[1]
        gbc_ref[:, :state] = (b_sum + dot(dk, c, 1, 0)).astype(gbc_ref.dtype)
        gbc_ref[:, state:] = (c_sum + dot(dk, b, 0, 0)).astype(gbc_ref.dtype)


def shards(layer_input, projection, ssm_input, step_logit, decay_rate, output_grad):
    tokens, x_rows, logit, grad_rows = layer_input[0], ssm_input[0], step_logit[0], output_grad[0]
    length, full = x_rows.shape
    heads = logit.shape[1]
    size = full // heads
    state = projection.shape[1] // 2
    groups = heads // HEADS
    width = HEADS * size
    count = lax.axis_size("seq")
    projected = jnp.dot(tokens, projection, preferred_element_type=F32).astype(BF16)
    b_rows, c_rows = projected[:, :state], projected[:, state:]
    dt = jax.nn.softplus(logit)
    log_decay = jnp.cumsum(-decay_rate[None, :] * dt, axis=0)
    to_end = jnp.exp(log_decay[-1][None, :] - log_decay)
    grow = jnp.exp(log_decay)
    span = grow[-1]

    def by_group(value):
        return value.reshape(length, groups, HEADS).transpose(1, 0, 2)

    cols = jnp.concatenate([by_group(v) for v in (log_decay, dt, to_end, grow)], axis=2)
    span_rows = jnp.broadcast_to(
        jnp.broadcast_to(span.reshape(groups, 1, HEADS, 1), (groups, 1, HEADS, size)).reshape(
            groups, 1, width
        ),
        (groups, 8, width),
    )
    whole = lambda shape: pl.BlockSpec(shape, lambda i: (0,) * len(shape))
    lanes = pl.BlockSpec((length, width), lambda i: (0, i))
    slab = lambda *shape: pl.BlockSpec((1,) + shape, lambda i: (i, 0, 0))
    limit = 60 * 2**20
    states = jax.ShapeDtypeStruct((groups, state, width), F32)
    local_state, local_adjoint = pl.pallas_call(
        functools.partial(local_kernel, size),
        grid=(groups,),
        in_specs=[
            whole((length, state)), whole((length, state)), lanes, lanes,
            slab(length, 4 * HEADS),
        ],
        out_specs=[slab(state, width), slab(state, width)],
        out_shape=[states, states],
        name="local_states",
    )(b_rows, c_rows, x_rows, grad_rows, cols)

    half = jax.ShapeDtypeStruct((groups, state, width), BF16)
    vmem = pl.BlockSpec(memory_space=pltpu.VMEM)
    slots = pltpu.VMEM((groups, state, width), F32)
    entering, leaving = pl.pallas_call(
        functools.partial(scan_kernel, count),
        in_specs=[vmem] * 3,
        out_specs=[vmem] * 2,
        out_shape=[half, half],
        scratch_shapes=[pltpu.VMEM((groups, 8, width), F32)]
        + [slots] * 6
        + [pltpu.SemaphoreType.DMA((2, 1))]
        + [pltpu.SemaphoreType.DMA((2, groups))] * 4,
        compiler_params=pltpu.CompilerParams(
            collective_id=0, has_side_effects=True, vmem_limit_bytes=limit
        ),
        name="scan_states",
    )(span_rows, local_state, local_adjoint)

    grad_x, row_sums, col_sums, inner, grad_bc = pl.pallas_call(
        functools.partial(grad_kernel, size),
        grid=(groups,),
        in_specs=[
            whole((length, state)), whole((length, state)), lanes, lanes,
            slab(length, 4 * HEADS), pl.BlockSpec((HEADS, length), lambda i: (i, 0)),
            slab(state, width), slab(state, width),
        ],
        out_specs=[
            lanes, pl.BlockSpec((HEADS, length), lambda i: (i, 0)), slab(length, 128),
            slab(1, width), whole((length, 2 * state)),
        ],
        out_shape=[
            jax.ShapeDtypeStruct((length, full), BF16),
            jax.ShapeDtypeStruct((heads, length), F32),
            jax.ShapeDtypeStruct((groups, length, 128), F32),
            jax.ShapeDtypeStruct((groups, 1, width), F32),
            jax.ShapeDtypeStruct((length, 2 * state), BF16),
        ],
        scratch_shapes=[
            pltpu.VMEM((length, length), F32), pltpu.VMEM((length, length), F32),
            pltpu.VMEM((length, state), F32), pltpu.VMEM((length, state), F32),
        ],
        name="gradients",
    )(b_rows, c_rows, x_rows, grad_rows, cols, log_decay.T, entering, leaving)

    def head_columns(part):
        piece = col_sums[:, :, part * HEADS : (part + 1) * HEADS]
        return piece.transpose(1, 0, 2).reshape(length, heads)

    inside, x_in, g_in = head_columns(0), head_columns(1), head_columns(2)
    both = span * jnp.sum(inner.reshape(heads, size), axis=1)
    position = jnp.arange(length)
    earlier = (position[:, None] > position[None, :]).astype(F32)
    change = g_in + row_sums.T - dt * inside
    d_log = (
        both[None, :]
        + jnp.dot(earlier, dt * x_in, precision=lax.Precision.HIGHEST)
        + jnp.dot((position[:, None] <= position[None, :]).astype(F32), change, precision=lax.Precision.HIGHEST)
    )
    d_dt = inside + x_in - decay_rate[None, :] * d_log
    grad_logit = d_dt * jax.nn.sigmoid(logit)
    grad_rate = -jnp.sum(dt * d_log, axis=0)
    group_rows = lax.psum_scatter(
        dot(tokens, grad_bc, 0, 0), "seq", scatter_dimension=0, tiled=True
    )
    weight_rows = lax.psum(group_rows, "dp")
    rate_sum = lax.psum(grad_rate, ("seq", "dp"))
    return (grad_x[None], grad_logit[None], rate_sum, weight_rows)


def solution(mesh):
    placed = (
        P("dp", "seq", None),
        P(),
        P("dp", "seq", None),
        P("dp", "seq", None),
        P(),
        P("dp", "seq", None),
    )
    return jax.shard_map(
        shards,
        mesh=mesh,
        in_specs=placed,
        out_specs=(P("dp", "seq", None), P("dp", "seq", None), P(), P("seq", None)),
        check_vma=False,
    )
```

```python
import functools

import jax
import jax.numpy as jnp
from jax import lax
from jax.experimental import pallas as pl
from jax.experimental.pallas import tpu as pltpu
from jax.sharding import PartitionSpec as P

F32 = jnp.float32
BF16 = jnp.bfloat16
HEADS = 8


def dot(a, b, ca, cb):
    return lax.dot_general(a, b, (((ca,), (cb,)), ((), ())), preferred_element_type=F32)


def pair_columns(cols, j, size):
    rows = cols.shape[0]
    lane = lax.broadcasted_iota(jnp.int32, (rows, 2 * size), 1)
    return jnp.where(lane < size, cols[:, j : j + 1], cols[:, j + 1 : j + 2])


def local_kernel(size, b_ref, c_ref, x_ref, g_ref, col_ref, s_ref, a_ref):
    cols = col_ref[0]
    width = 2 * size
    for pair in range(HEADS // 2):
        lanes = pl.ds(pair * width, width)
        j = 2 * pair
        to_end = pair_columns(cols, j + HEADS, size) * pair_columns(cols, j + 2 * HEADS, size)
        grow = pair_columns(cols, j + 3 * HEADS, size)
        xs = (x_ref[:, lanes].astype(F32) * to_end).astype(BF16)
        gs = (g_ref[:, lanes].astype(F32) * grow).astype(BF16)
        s_ref[0, :, lanes] = dot(b_ref[...], xs, 0, 0)
        a_ref[0, :, lanes] = dot(c_ref[...], gs, 0, 0)


def scan_kernel(
    n, d_ref, s_ref, a_ref, e_out, f_out,
    d_in, s_in, a_in, e_in, f_in, e_snd, f_snd,
    d_sem, s_sem, a_sem, e_sem, f_sem,
):
    chunks = s_ref.shape[0]
    nz = n // 2
    me = lax.axis_index("seq")
    odd = lax.rem(me, 2)
    z = lax.div(me, 2)
    partner = me + 1 - 2 * odd
    first, last = z == 0, z == nz - 1
    barrier = pltpu.get_barrier_semaphore()

    def greet(who):
        pl.semaphore_signal(
            barrier, inc=1, device_id={"seq": who}, device_id_type=pl.DeviceIdType.MESH
        )

    greet(partner)
    pl.when(jnp.logical_not(first))(lambda: greet(me - 2))
    pl.when(jnp.logical_not(last))(lambda: greet(me + 2))
    end = jnp.logical_or(first, last)
    pl.when(end)(lambda: pl.semaphore_wait(barrier, min(nz, 2)))
    pl.when(jnp.logical_not(end))(lambda: pl.semaphore_wait(barrier, 3))

    def send(src, dst, sems, k, who):
        return pltpu.make_async_remote_copy(
            src_ref=src, dst_ref=dst, send_sem=sems.at[0, k], recv_sem=sems.at[1, k],
            device_id={"seq": who}, device_id_type=pl.DeviceIdType.MESH,
        )

    def copy_d():
        return send(d_ref, d_in, d_sem, 0, partner)

    def copy_s(k):
        return send(s_ref.at[k], s_in.at[k], s_sem, k, partner)

    def copy_a(k):
        return send(a_ref.at[k], a_in.at[k], a_sem, k, partner)

    def copy_e(k):
        return send(e_snd.at[k], e_in.at[k], e_sem, k, me + 2)

    def copy_f(k):
        return send(f_snd.at[k], f_in.at[k], f_sem, k, me - 2)

    copy_d().start()
    for k in range(chunks):
        copy_s(k).start()
        copy_a(k).start()

    @pl.when(first)
    def _():
        e_in[...] = jnp.zeros_like(e_in)

    @pl.when(last)
    def _():
        f_in[...] = jnp.zeros_like(f_in)

    copy_d().wait_recv()

    def advance(k, near, far, carry, out, snd, near_first):
        @pl.when(near_first)
        def _():
            value = carry[k]
            out[k] = value.astype(out.dtype)
            middle = d_ref[k, 0:1] * value + near[k]
            snd[k] = d_in[k, 0:1] * middle + far[k]

        @pl.when(jnp.logical_not(near_first))
        def _():
            middle = d_in[k, 0:1] * carry[k] + far[k]
            out[k] = middle.astype(out.dtype)
            snd[k] = d_ref[k, 0:1] * middle + near[k]

    def step(t, unused):
        kf = t - z

        @pl.when(jnp.logical_and(kf >= 0, kf < chunks))
        def _():
            copy_s(kf).wait_recv()
            pl.when(jnp.logical_not(first))(lambda: copy_e(kf).wait_recv())
            advance(kf, s_ref, s_in, e_in, e_out, e_snd, odd == 0)
            pl.when(jnp.logical_not(last))(lambda: copy_e(kf).start())

        kb = t - (nz - 1 - z)

        @pl.when(jnp.logical_and(kb >= 0, kb < chunks))
        def _():
            copy_a(kb).wait_recv()
            pl.when(jnp.logical_not(last))(lambda: copy_f(kb).wait_recv())
            advance(kb, a_ref, a_in, f_in, f_out, f_snd, odd == 1)
            pl.when(jnp.logical_not(first))(lambda: copy_f(kb).start())

        return unused

    lax.fori_loop(0, chunks + nz - 1, step, 0)
    copy_d().wait_send()
    for k in range(chunks):
        copy_s(k).wait_send()
        copy_a(k).wait_send()

    @pl.when(jnp.logical_not(last))
    def _():
        for k in range(chunks):
            copy_e(k).wait_send()

    @pl.when(jnp.logical_not(first))
    def _():
        for k in range(chunks):
            copy_f(k).wait_send()


def grad_kernel(
    size, b_ref, c_ref, x_ref, g_ref, col_ref, row_ref, e_ref, f_ref,
    dx_ref, rows_ref, cols_ref, ef_ref, gbc_ref,
    scores, d_scores, d_b, d_c,
):
    group = pl.program_id(0)
    b, c = b_ref[...], c_ref[...]
    length = b.shape[0]
    width = 2 * size

    @pl.when(group == 0)
    def _():
        scores[...] = dot(b, c, 1, 1)
        d_scores[...] = jnp.zeros_like(d_scores)
        d_b[...] = jnp.zeros_like(d_b)
        d_c[...] = jnp.zeros_like(d_c)

    cols = col_ref[0]
    rows = row_ref[...]
    k_st = scores[...]
    causal = lax.broadcasted_iota(jnp.int32, (length, length), 1) >= lax.broadcasted_iota(
        jnp.int32, (length, length), 0
    )
    lane = lax.broadcasted_iota(jnp.int32, (length, width), 1)
    low = lane < size
    place = lax.broadcasted_iota(jnp.int32, (length, cols_ref.shape[2]), 1)
    result = jnp.zeros((length, cols_ref.shape[2]), F32)
    q_sum = d_scores[...]
    b_sum, c_sum = d_b[...], d_c[...]
    for pair in range(HEADS // 2):
        lanes = pl.ds(pair * width, width)
        x2, g2 = x_ref[:, lanes], g_ref[:, lanes]
        x2f, g2f = x2.astype(F32), g2.astype(F32)
        e2, f2 = e_ref[0, :, lanes], f_ref[0, :, lanes]
        j = 2 * pair
        dt2 = pair_columns(cols, j + HEADS, size)
        end2 = pair_columns(cols, j + 2 * HEADS, size)
        grow2 = pair_columns(cols, j + 3 * HEADS, size)
        g_low = jnp.where(low, g2, jnp.zeros_like(g2))
        g_high = jnp.where(low, jnp.zeros_like(g2), g2)
        g_both = jnp.concatenate([g_low, g_high], axis=0)
        gram = dot(x2, g_both, 1, 1)
        weights = []
        for side in range(2):
            h = j + side
            gap = rows[h : h + 1, :] - cols[:, h : h + 1]
            decay = jnp.exp(jnp.where(causal, gap, -jnp.inf))
            mg = decay * gram[:, side * length : (side + 1) * length]
            dt = cols[:, h + HEADS : h + HEADS + 1]
            q_sum = q_sum + mg * dt
            raw = mg * k_st
            rows_ref[h : h + 1, :] = jnp.sum(raw * dt, axis=0, keepdims=True)
            result = jnp.where(place == h, jnp.sum(raw, axis=1, keepdims=True), result)
            weights.append((decay * k_st).astype(BF16))
        z2 = dot(jnp.concatenate(weights, axis=1), g_both, 1, 0)
        z_in = dot(b, f2, 1, 0) * end2
        dx_ref[:, lanes] = (dt2 * (z2 + z_in)).astype(dx_ref.dtype)
        y_in = dot(c, e2, 1, 0) * grow2
        xz, gy = x2f * z_in, g2f * y_in
        zero = jnp.zeros_like(xz)
        for side in range(2):
            h = j + side
            mask = low if side == 0 else jnp.logical_not(low)
            xs = jnp.sum(jnp.where(mask, xz, zero), axis=1, keepdims=True)
            gs = jnp.sum(jnp.where(mask, gy, zero), axis=1, keepdims=True)
            result = jnp.where(place == h + HEADS, xs, result)
            result = jnp.where(place == h + 2 * HEADS, gs, result)
        ef_ref[0, :, lanes] = jnp.sum(e2.astype(F32) * f2.astype(F32), axis=0, keepdims=True)
        b_sum = b_sum + dot((x2f * (end2 * dt2)).astype(BF16), f2, 1, 1)
        c_sum = c_sum + dot((g2f * grow2).astype(BF16), e2, 1, 1)
    cols_ref[0] = result
    d_scores[...] = q_sum
    d_b[...] = b_sum
    d_c[...] = c_sum

    @pl.when(group == pl.num_programs(0) - 1)
    def _():
        dk = q_sum.astype(BF16)
        state = b.shape[1]
        gbc_ref[:, :state] = (b_sum + dot(dk, c, 1, 0)).astype(gbc_ref.dtype)
        gbc_ref[:, state:] = (c_sum + dot(dk, b, 0, 0)).astype(gbc_ref.dtype)


def reversed_bits(value, size):
    out, left = 0, size
    while left > 1:
        out, value, left = 2 * out + value % 2, value // 2, left // 2
    return out


def weight_kernel(
    n, m, t_ref, g_ref, rate_ref, out_ref, rate_out,
    acc, got, ring, r_acc, r_got, sem, out_sem, r_sem,
):
    chunks, blocks, rows = acc.shape[0], acc.shape[1], acc.shape[2]
    piece = chunks * rows
    seq, dp = lax.axis_index("seq"), lax.axis_index("dp")
    steps, bit = [], 1
    while bit < m:
        steps.append(("dp", bit, lax.rem(lax.div(dp, bit), 2)))
        bit *= 2
    bit = 1
    while bit < n:
        steps.append(("seq", bit, lax.rem(lax.div(seq, bit), 2)))
        bit *= 2
    count = len(steps)

    def peer(s):
        axis, bit, mine = steps[s]
        return {axis: lax.axis_index(axis) + bit - 2 * bit * mine}

    def dp_peer(k):
        other, bit = dp, 1
        while bit < m:
            if k & bit:
                other = other + bit - 2 * bit * lax.rem(lax.div(dp, bit), 2)
            bit *= 2
        return {"dp": other}

    barrier = pltpu.get_barrier_semaphore()
    friends = [dp_peer(k) for k in range(1, m)] + [
        peer(s) for s in range(count) if steps[s][0] == "seq"
    ]
    for friend in friends:
        pl.semaphore_signal(
            barrier, inc=1, device_id=friend, device_id_type=pl.DeviceIdType.MESH
        )

    starts, base, width = [], 0, blocks
    for s in range(count):
        width //= 2
        mine = steps[s][2]
        starts.append((base + width * mine, base + width * (1 - mine), width))
        base = base + width * mine
    offsets, total = [], 0
    for s in range(count):
        offsets.append(total)
        total += starts[s][2]

    def copy(c, s):
        keep, give, size = starts[s]
        return pltpu.make_async_remote_copy(
            src_ref=acc.at[c, pl.ds(give, size)],
            dst_ref=got.at[c, pl.ds(offsets[s], size)],
            send_sem=sem.at[0, c, s], recv_sem=sem.at[1, c, s],
            device_id=peer(s), device_id_type=pl.DeviceIdType.MESH,
        )

    def rate_copy(s):
        return pltpu.make_async_remote_copy(
            src_ref=r_acc.at[s], dst_ref=r_got.at[s],
            send_sem=r_sem.at[0, s], recv_sem=r_sem.at[1, s],
            device_id=peer(s), device_id_type=pl.DeviceIdType.MESH,
        )

    def out_copy(c, k):
        return pltpu.make_async_remote_copy(
            src_ref=ring.at[0, c], dst_ref=ring.at[k, c],
            send_sem=out_sem.at[0, c, k], recv_sem=out_sem.at[1, c, k],
            device_id=dp_peer(k), device_id_type=pl.DeviceIdType.MESH,
        )

    g = g_ref[...]
    r_acc[0] = rate_ref[...]
    block = 128
    for first in range(0, t_ref.shape[1], block):
        product = dot(t_ref[:, first : first + block], g, 0, 0)
        for part in range(0, block, rows):
            row = first + part
            owner, inner = row // (m * piece), row % (m * piece)
            place = reversed_bits(inner // piece, m) * n + reversed_bits(owner, n)
            acc[inner % piece // rows, place] = product[part : part + rows]
    pl.semaphore_wait(barrier, len(friends))
    for c in range(chunks):
        copy(c, 0).start()
    rate_copy(0).start()
    for turn in range(chunks + count):
        for c in range(chunks):
            s = turn - c
            if not 0 <= s < count:
                continue
            copy(c, s).wait_recv()
            keep, give, size = starts[s]
            value = acc[c, pl.ds(keep, size)] + got[c, pl.ds(offsets[s], size)]
            if s + 1 < count:
                acc[c, pl.ds(keep, size)] = value
                copy(c, s + 1).start()
            else:
                ring[0, c] = value[0]
                for k in range(1, m):
                    out_copy(c, k).start()
        if turn < count:
            rate_copy(turn).wait_recv()
            r_acc[turn + 1] = r_acc[turn] + r_got[turn]
            if turn + 1 < count:
                rate_copy(turn + 1).start()
    rate_out[...] = r_acc[count]
    for c in range(chunks):
        for k in range(m):
            if k > 0:
                out_copy(c, k).wait_recv()
            where = dp_peer(k)["dp"] if k > 0 else dp
            out_ref[pl.ds(where * piece + c * rows, rows)] = ring[k, c]
    for c in range(chunks):
        for s in range(count):
            copy(c, s).wait_send()
        for k in range(1, m):
            out_copy(c, k).wait_send()
    for s in range(count):
        rate_copy(s).wait_send()


def shards(layer_input, projection, ssm_input, step_logit, decay_rate, output_grad):
    tokens, x_rows, logit, grad_rows = layer_input[0], ssm_input[0], step_logit[0], output_grad[0]
    length, full = x_rows.shape
    heads = logit.shape[1]
    size = full // heads
    state = projection.shape[1] // 2
    groups = heads // HEADS
    width = HEADS * size
    count = lax.axis_size("seq")
    projected = jnp.dot(tokens, projection, preferred_element_type=F32).astype(BF16)
    b_rows, c_rows = projected[:, :state], projected[:, state:]
    dt = jax.nn.softplus(logit)
    log_decay = jnp.cumsum(-decay_rate[None, :] * dt, axis=0)
    to_end = jnp.exp(log_decay[-1][None, :] - log_decay)
    grow = jnp.exp(log_decay)
    span = grow[-1]

    def by_group(value):
        return value.reshape(length, groups, HEADS).transpose(1, 0, 2)

    cols = jnp.concatenate([by_group(v) for v in (log_decay, dt, to_end, grow)], axis=2)
    span_rows = jnp.broadcast_to(
        jnp.broadcast_to(span.reshape(groups, 1, HEADS, 1), (groups, 1, HEADS, size)).reshape(
            groups, 1, width
        ),
        (groups, 8, width),
    )
    whole = lambda shape: pl.BlockSpec(shape, lambda i: (0,) * len(shape))
    lanes = pl.BlockSpec((length, width), lambda i: (0, i))
    slab = lambda *shape: pl.BlockSpec((1,) + shape, lambda i: (i, 0, 0))
    limit = 60 * 2**20
    states = jax.ShapeDtypeStruct((groups, state, width), F32)
    local_state, local_adjoint = pl.pallas_call(
        functools.partial(local_kernel, size),
        grid=(groups,),
        in_specs=[
            whole((length, state)), whole((length, state)), lanes, lanes,
            slab(length, 4 * HEADS),
        ],
        out_specs=[slab(state, width), slab(state, width)],
        out_shape=[states, states],
        name="local_states",
    )(b_rows, c_rows, x_rows, grad_rows, cols)

    half = jax.ShapeDtypeStruct((groups, state, width), BF16)
    vmem = pl.BlockSpec(memory_space=pltpu.VMEM)
    slots = pltpu.VMEM((groups, state, width), F32)
    entering, leaving = pl.pallas_call(
        functools.partial(scan_kernel, count),
        in_specs=[vmem] * 3,
        out_specs=[vmem] * 2,
        out_shape=[half, half],
        scratch_shapes=[pltpu.VMEM((groups, 8, width), F32)]
        + [slots] * 6
        + [pltpu.SemaphoreType.DMA((2, 1))]
        + [pltpu.SemaphoreType.DMA((2, groups))] * 4,
        compiler_params=pltpu.CompilerParams(
            collective_id=0, has_side_effects=True, vmem_limit_bytes=limit
        ),
        name="scan_states",
    )(span_rows, local_state, local_adjoint)

    grad_x, row_sums, col_sums, inner, grad_bc = pl.pallas_call(
        functools.partial(grad_kernel, size),
        grid=(groups,),
        in_specs=[
            whole((length, state)), whole((length, state)), lanes, lanes,
            slab(length, 4 * HEADS), pl.BlockSpec((HEADS, length), lambda i: (i, 0)),
            slab(state, width), slab(state, width),
        ],
        out_specs=[
            lanes, pl.BlockSpec((HEADS, length), lambda i: (i, 0)), slab(length, 128),
            slab(1, width), whole((length, 2 * state)),
        ],
        out_shape=[
            jax.ShapeDtypeStruct((length, full), BF16),
            jax.ShapeDtypeStruct((heads, length), F32),
            jax.ShapeDtypeStruct((groups, length, 128), F32),
            jax.ShapeDtypeStruct((groups, 1, width), F32),
            jax.ShapeDtypeStruct((length, 2 * state), BF16),
        ],
        scratch_shapes=[
            pltpu.VMEM((length, length), F32), pltpu.VMEM((length, length), F32),
            pltpu.VMEM((length, state), F32), pltpu.VMEM((length, state), F32),
        ],
        name="gradients",
    )(b_rows, c_rows, x_rows, grad_rows, cols, log_decay.T, entering, leaving)

    def head_columns(part):
        piece = col_sums[:, :, part * HEADS : (part + 1) * HEADS]
        return piece.transpose(1, 0, 2).reshape(length, heads)

    inside, x_in, g_in = head_columns(0), head_columns(1), head_columns(2)
    both = span * jnp.sum(inner.reshape(heads, size), axis=1)
    position = jnp.arange(length)
    earlier = (position[:, None] > position[None, :]).astype(F32)
    change = g_in + row_sums.T - dt * inside
    d_log = (
        both[None, :]
        + jnp.dot(earlier, dt * x_in, precision=lax.Precision.HIGHEST)
        + jnp.dot((position[:, None] <= position[None, :]).astype(F32), change, precision=lax.Precision.HIGHEST)
    )
    d_dt = inside + x_in - decay_rate[None, :] * d_log
    grad_logit = d_dt * jax.nn.sigmoid(logit)
    grad_rate = -jnp.sum(dt * d_log, axis=0)
    members = lax.axis_size("dp")
    blocks = count * members
    piece = tokens.shape[1] // blocks
    chunks = max(1, min(4, piece // 8))
    rows = piece // chunks
    levels = blocks.bit_length() - 1
    rate_rows = jnp.pad(grad_rate.reshape(1, heads), ((0, 7), (0, 128 - heads)))
    weight_rows, rate_sum = pl.pallas_call(
        functools.partial(weight_kernel, count, members),
        in_specs=[vmem] * 3,
        out_specs=[vmem] * 2,
        out_shape=[
            jax.ShapeDtypeStruct((members * piece, 2 * state), F32),
            jax.ShapeDtypeStruct((8, 128), F32),
        ],
        scratch_shapes=[
            pltpu.VMEM((chunks, blocks, rows, 2 * state), F32),
            pltpu.VMEM((chunks, blocks, rows, 2 * state), F32),
            pltpu.VMEM((members, chunks, rows, 2 * state), F32),
            pltpu.VMEM((levels + 1, 8, 128), F32),
            pltpu.VMEM((levels, 8, 128), F32),
            pltpu.SemaphoreType.DMA((2, chunks, levels)),
            pltpu.SemaphoreType.DMA((2, chunks, members)),
            pltpu.SemaphoreType.DMA((2, levels)),
        ],
        compiler_params=pltpu.CompilerParams(
            collective_id=1, has_side_effects=True, vmem_limit_bytes=limit
        ),
        name="weight_gradient",
    )(tokens, grad_bc, rate_rows)
    rate_sum = rate_sum[0, :heads]
    return (grad_x[None], grad_logit[None], rate_sum, weight_rows)


def solution(mesh):
    placed = (
        P("dp", "seq", None),
        P(),
        P("dp", "seq", None),
        P("dp", "seq", None),
        P(),
        P("dp", "seq", None),
    )
    return jax.shard_map(
        shards,
        mesh=mesh,
        in_specs=placed,
        out_specs=(P("dp", "seq", None), P("dp", "seq", None), P(), P("seq", None)),
        check_vma=False,
    )
```

```python
import functools

import jax
import jax.numpy as jnp
from jax import lax
from jax.experimental import pallas as pl
from jax.experimental.pallas import tpu as pltpu
from jax.sharding import PartitionSpec as P

F32 = jnp.float32
BF16 = jnp.bfloat16
HEADS = 4


def dot(a, b, ca, cb):
    return lax.dot_general(a, b, (((ca,), (cb,)), ((), ())), preferred_element_type=F32)


def pair_columns(cols, j, size):
    rows = cols.shape[0]
    lane = lax.broadcasted_iota(jnp.int32, (rows, 2 * size), 1)
    return jnp.where(lane < size, cols[:, j : j + 1], cols[:, j + 1 : j + 2])


def layer_kernel(
    n, size, b_ref, c_ref, x_ref, g_ref, col_ref, row_ref, d_ref,
    dx_ref, rows_ref, cols_ref, ef_ref, gbc_ref,
    s_ref, a_ref, e_out, f_out, scores, d_scores, d_b, d_c,
    d_in, s_in, a_in, e_in, f_in, e_snd, f_snd,
    d_sem, s_sem, a_sem, e_sem, f_sem,
):
    chunks = s_ref.shape[0]
    length = b_ref.shape[0]
    state = b_ref.shape[1]
    width = 2 * size
    heads = chunks * HEADS
    nz = n // 2
    me = lax.axis_index("seq")
    odd = lax.rem(me, 2)
    z = lax.div(me, 2)
    partner = me + 1 - 2 * odd
    first, last = z == 0, z == nz - 1
    barrier = pltpu.get_barrier_semaphore()

    def greet(who):
        pl.semaphore_signal(
            barrier, inc=1, device_id={"seq": who}, device_id_type=pl.DeviceIdType.MESH
        )

    greet(partner)
    pl.when(jnp.logical_not(first))(lambda: greet(me - 2))
    pl.when(jnp.logical_not(last))(lambda: greet(me + 2))

    def send(src, dst, sems, k, who):
        return pltpu.make_async_remote_copy(
            src_ref=src, dst_ref=dst, send_sem=sems.at[0, k], recv_sem=sems.at[1, k],
            device_id={"seq": who}, device_id_type=pl.DeviceIdType.MESH,
        )

    def copy_d():
        return send(d_ref, d_in, d_sem, 0, partner)

    def copy_s(k):
        return send(s_ref.at[k], s_in.at[k], s_sem, k, partner)

    def copy_a(k):
        return send(a_ref.at[k], a_in.at[k], a_sem, k, partner)

    def copy_e(k):
        return send(e_snd.at[k], e_in.at[k], e_sem, k, me + 2)

    def copy_f(k):
        return send(f_snd.at[k], f_in.at[k], f_sem, k, me - 2)

    def pair_lanes(k, pair):
        return pl.ds(pl.multiple_of(k * (HEADS * size) + pair * width, width), width)

    def local(k, unused):
        cols = col_ref[k]
        for pair in range(HEADS // 2):
            lanes = pl.ds(pair * width, width)
            wide = pair_lanes(k, pair)
            j = 2 * pair
            to_end = pair_columns(cols, j + HEADS, size) * pair_columns(cols, j + 2 * HEADS, size)
            grow = pair_columns(cols, j + 3 * HEADS, size)
            xs = (x_ref[:, wide].astype(F32) * to_end).astype(BF16)
            gs = (g_ref[:, wide].astype(F32) * grow).astype(BF16)
            s_ref[k, :, lanes] = dot(b_ref[...], xs, 0, 0)
            a_ref[k, :, lanes] = dot(c_ref[...], gs, 0, 0)

        @pl.when(k > 0)
        def _():
            copy_s(k - 1).start()
            copy_a(k - 1).start()

        return unused

    end = jnp.logical_or(first, last)
    pl.when(end)(lambda: pl.semaphore_wait(barrier, min(nz, 2)))
    pl.when(jnp.logical_not(end))(lambda: pl.semaphore_wait(barrier, 3))
    copy_d().start()
    lax.fori_loop(0, chunks, local, 0)
    copy_s(chunks - 1).start()
    copy_a(chunks - 1).start()

    @pl.when(first)
    def _():
        e_in[...] = jnp.zeros_like(e_in)

    @pl.when(last)
    def _():
        f_in[...] = jnp.zeros_like(f_in)

    b, c = b_ref[...], c_ref[...]
    scores[...] = dot(b, c, 1, 1)
    d_scores[...] = jnp.zeros_like(d_scores)
    d_b[...] = jnp.zeros_like(d_b)
    d_c[...] = jnp.zeros_like(d_c)
    cols_ref[...] = jnp.zeros_like(cols_ref)
    copy_d().wait_recv()

    def advance(k, near, far, carry, out, snd, near_first):
        @pl.when(near_first)
        def _():
            value = carry[k]
            out[k] = value.astype(out.dtype)
            middle = d_ref[k, 0:1] * value + near[k]
            snd[k] = d_in[k, 0:1] * middle + far[k]

        @pl.when(jnp.logical_not(near_first))
        def _():
            middle = d_in[k, 0:1] * carry[k] + far[k]
            out[k] = middle.astype(out.dtype)
            snd[k] = d_ref[k, 0:1] * middle + near[k]

    def gradients(k):
        cols = col_ref[k]
        rows = row_ref[k]
        k_st = scores[...]
        causal = lax.broadcasted_iota(jnp.int32, (length, length), 1) >= lax.broadcasted_iota(
            jnp.int32, (length, length), 0
        )
        low = lax.broadcasted_iota(jnp.int32, (length, width), 1) < size
        place = lax.broadcasted_iota(jnp.int32, cols_ref.shape, 1) - k * HEADS
        result = cols_ref[...]
        q_sum = d_scores[...]
        b_sum, c_sum = d_b[...], d_c[...]
        for pair in range(HEADS // 2):
            lanes = pl.ds(pair * width, width)
            wide = pair_lanes(k, pair)
            x2, g2 = x_ref[:, wide], g_ref[:, wide]
            x2f, g2f = x2.astype(F32), g2.astype(F32)
            e2, f2 = e_out[k, :, lanes], f_out[k, :, lanes]
            j = 2 * pair
            dt2 = pair_columns(cols, j + HEADS, size)
            end2 = pair_columns(cols, j + 2 * HEADS, size)
            grow2 = pair_columns(cols, j + 3 * HEADS, size)
            g_low = jnp.where(low, g2, jnp.zeros_like(g2))
            g_high = jnp.where(low, jnp.zeros_like(g2), g2)
            g_both = jnp.concatenate([g_low, g_high], axis=0)
            gram = dot(x2, g_both, 1, 1)
            weights = []
            for side in range(2):
                h = j + side
                gap = rows[h : h + 1, :] - cols[:, h : h + 1]
                decay = jnp.exp(jnp.where(causal, gap, -jnp.inf))
                mg = decay * gram[:, side * length : (side + 1) * length]
                dt = cols[:, h + HEADS : h + HEADS + 1]
                q_sum = q_sum + mg * dt
                raw = mg * k_st
                rows_ref[k, h : h + 1, :] = jnp.sum(raw * dt, axis=0, keepdims=True)
                result = jnp.where(place == h, jnp.sum(raw, axis=1, keepdims=True), result)
                weights.append((decay * k_st).astype(BF16))
            z2 = dot(jnp.concatenate(weights, axis=1), g_both, 1, 0)
            z_in = dot(b, f2, 1, 0) * end2
            dx_ref[:, wide] = (dt2 * (z2 + z_in)).astype(dx_ref.dtype)
            y_in = dot(c, e2, 1, 0) * grow2
            xz, gy = x2f * z_in, g2f * y_in
            zero = jnp.zeros_like(xz)
            for side in range(2):
                h = j + side
                mask = low if side == 0 else jnp.logical_not(low)
                xs = jnp.sum(jnp.where(mask, xz, zero), axis=1, keepdims=True)
                gs = jnp.sum(jnp.where(mask, gy, zero), axis=1, keepdims=True)
                result = jnp.where(place == h + heads, xs, result)
                result = jnp.where(place == h + 2 * heads, gs, result)
            ef_ref[k, :, lanes] = jnp.sum(
                e2.astype(F32) * f2.astype(F32), axis=0, keepdims=True
            )
            b_sum = b_sum + dot((x2f * (end2 * dt2)).astype(BF16), f2, 1, 1)
            c_sum = c_sum + dot((g2f * grow2).astype(BF16), e2, 1, 1)
        cols_ref[...] = result
        d_scores[...] = q_sum
        d_b[...] = b_sum
        d_c[...] = c_sum

    def step(t, unused):
        kf = t - z

        @pl.when(jnp.logical_and(kf >= 0, kf < chunks))
        def _():
            copy_s(kf).wait_recv()
            pl.when(jnp.logical_not(first))(lambda: copy_e(kf).wait_recv())
            advance(kf, s_ref, s_in, e_in, e_out, e_snd, odd == 0)
            pl.when(jnp.logical_not(last))(lambda: copy_e(kf).start())

        kb = t - (nz - 1 - z)

        @pl.when(jnp.logical_and(kb >= 0, kb < chunks))
        def _():
            copy_a(kb).wait_recv()
            pl.when(jnp.logical_not(last))(lambda: copy_f(kb).wait_recv())
            advance(kb, a_ref, a_in, f_in, f_out, f_snd, odd == 1)
            pl.when(jnp.logical_not(first))(lambda: copy_f(kb).start())

        pl.when(t >= nz - 1)(lambda: gradients(t - (nz - 1)))
        return unused

    lax.fori_loop(0, chunks + nz - 1, step, 0)
    dk = d_scores[...].astype(BF16)
    gbc_ref[:, :state] = (d_b[...] + dot(dk, c, 1, 0)).astype(gbc_ref.dtype)
    gbc_ref[:, state:] = (d_c[...] + dot(dk, b, 0, 0)).astype(gbc_ref.dtype)
    copy_d().wait_send()

    def settle(k, unused):
        copy_s(k).wait_send()
        copy_a(k).wait_send()
        pl.when(jnp.logical_not(last))(lambda: copy_e(k).wait_send())
        pl.when(jnp.logical_not(first))(lambda: copy_f(k).wait_send())
        return unused

    lax.fori_loop(0, chunks, settle, 0)


def reversed_bits(value, size):
    out, left = 0, size
    while left > 1:
        out, value, left = 2 * out + value % 2, value // 2, left // 2
    return out


def weight_kernel(
    n, m, t_ref, g_ref, rate_ref, out_ref, rate_out,
    acc, got, ring, r_acc, r_got, sem, out_sem, r_sem,
):
    chunks, blocks, rows = acc.shape[0], acc.shape[1], acc.shape[2]
    piece = chunks * rows
    seq, dp = lax.axis_index("seq"), lax.axis_index("dp")
    steps, bit = [], 1
    while bit < m:
        steps.append(("dp", bit, lax.rem(lax.div(dp, bit), 2)))
        bit *= 2
    bit = 1
    while bit < n:
        steps.append(("seq", bit, lax.rem(lax.div(seq, bit), 2)))
        bit *= 2
    count = len(steps)

    def peer(s):
        axis, bit, mine = steps[s]
        return {axis: lax.axis_index(axis) + bit - 2 * bit * mine}

    def dp_peer(k):
        other, bit = dp, 1
        while bit < m:
            if k & bit:
                other = other + bit - 2 * bit * lax.rem(lax.div(dp, bit), 2)
            bit *= 2
        return {"dp": other}

    barrier = pltpu.get_barrier_semaphore()
    friends = [dp_peer(k) for k in range(1, m)] + [
        peer(s) for s in range(count) if steps[s][0] == "seq"
    ]
    for friend in friends:
        pl.semaphore_signal(
            barrier, inc=1, device_id=friend, device_id_type=pl.DeviceIdType.MESH
        )

    starts, base, width = [], 0, blocks
    for s in range(count):
        width //= 2
        mine = steps[s][2]
        starts.append((base + width * mine, base + width * (1 - mine), width))
        base = base + width * mine
    offsets, total = [], 0
    for s in range(count):
        offsets.append(total)
        total += starts[s][2]

    def copy(c, s):
        keep, give, size = starts[s]
        return pltpu.make_async_remote_copy(
            src_ref=acc.at[c, pl.ds(give, size)],
            dst_ref=got.at[c, pl.ds(offsets[s], size)],
            send_sem=sem.at[0, c, s], recv_sem=sem.at[1, c, s],
            device_id=peer(s), device_id_type=pl.DeviceIdType.MESH,
        )

    def rate_copy(s):
        return pltpu.make_async_remote_copy(
            src_ref=r_acc.at[s], dst_ref=r_got.at[s],
            send_sem=r_sem.at[0, s], recv_sem=r_sem.at[1, s],
            device_id=peer(s), device_id_type=pl.DeviceIdType.MESH,
        )

    def out_copy(c, k):
        return pltpu.make_async_remote_copy(
            src_ref=ring.at[0, c], dst_ref=ring.at[k, c],
            send_sem=out_sem.at[0, c, k], recv_sem=out_sem.at[1, c, k],
            device_id=dp_peer(k), device_id_type=pl.DeviceIdType.MESH,
        )

    g = g_ref[...]
    r_acc[0] = rate_ref[...]
    block = 128
    for first in range(0, t_ref.shape[1], block):
        product = dot(t_ref[:, first : first + block], g, 0, 0)
        for part in range(0, block, rows):
            row = first + part
            owner, inner = row // (m * piece), row % (m * piece)
            place = reversed_bits(inner // piece, m) * n + reversed_bits(owner, n)
            acc[inner % piece // rows, place] = product[part : part + rows]
    pl.semaphore_wait(barrier, len(friends))
    for c in range(chunks):
        copy(c, 0).start()
    rate_copy(0).start()
    for turn in range(chunks + count):
        for c in range(chunks):
            s = turn - c
            if not 0 <= s < count:
                continue
            copy(c, s).wait_recv()
            keep, give, size = starts[s]
            value = acc[c, pl.ds(keep, size)] + got[c, pl.ds(offsets[s], size)]
            if s + 1 < count:
                acc[c, pl.ds(keep, size)] = value
                copy(c, s + 1).start()
            else:
                ring[0, c] = value[0]
                for k in range(1, m):
                    out_copy(c, k).start()
        if turn < count:
            rate_copy(turn).wait_recv()
            r_acc[turn + 1] = r_acc[turn] + r_got[turn]
            if turn + 1 < count:
                rate_copy(turn + 1).start()
    rate_out[...] = r_acc[count]
    for c in range(chunks):
        for k in range(m):
            if k > 0:
                out_copy(c, k).wait_recv()
            where = dp_peer(k)["dp"] if k > 0 else dp
            out_ref[pl.ds(where * piece + c * rows, rows)] = ring[k, c]
    for c in range(chunks):
        for s in range(count):
            copy(c, s).wait_send()
        for k in range(1, m):
            out_copy(c, k).wait_send()
    for s in range(count):
        rate_copy(s).wait_send()


def shards(layer_input, projection, ssm_input, step_logit, decay_rate, output_grad):
    tokens, x_rows, logit, grad_rows = layer_input[0], ssm_input[0], step_logit[0], output_grad[0]
    length, full = x_rows.shape
    heads = logit.shape[1]
    size = full // heads
    state = projection.shape[1] // 2
    groups = heads // HEADS
    width = HEADS * size
    count = lax.axis_size("seq")
    projected = jnp.dot(tokens, projection, preferred_element_type=F32).astype(BF16)
    b_rows, c_rows = projected[:, :state], projected[:, state:]
    dt = jax.nn.softplus(logit)
    log_decay = jnp.cumsum(-decay_rate[None, :] * dt, axis=0)
    to_end = jnp.exp(log_decay[-1][None, :] - log_decay)
    grow = jnp.exp(log_decay)
    span = grow[-1]

    def by_group(value):
        return value.reshape(length, groups, HEADS).transpose(1, 0, 2)

    cols = jnp.concatenate([by_group(v) for v in (log_decay, dt, to_end, grow)], axis=2)
    span_rows = jnp.broadcast_to(
        jnp.broadcast_to(span.reshape(groups, 1, HEADS, 1), (groups, 1, HEADS, size)).reshape(
            groups, 1, width
        ),
        (groups, 8, width),
    )
    limit = 60 * 2**20
    vmem = pl.BlockSpec(memory_space=pltpu.VMEM)
    slots = pltpu.VMEM((groups, state, width), F32)
    half = pltpu.VMEM((groups, state, width), BF16)
    square = pltpu.VMEM((length, length), F32)
    sums = pltpu.VMEM((length, state), F32)
    grad_x, row_sums, col_sums, inner, grad_bc = pl.pallas_call(
        functools.partial(layer_kernel, count, size),
        in_specs=[vmem] * 7,
        out_specs=[vmem] * 5,
        out_shape=[
            jax.ShapeDtypeStruct((length, full), BF16),
            jax.ShapeDtypeStruct((groups, HEADS, length), F32),
            jax.ShapeDtypeStruct((length, 3 * heads), F32),
            jax.ShapeDtypeStruct((groups, 1, width), F32),
            jax.ShapeDtypeStruct((length, 2 * state), BF16),
        ],
        scratch_shapes=[slots, slots, half, half, square, square, sums, sums]
        + [pltpu.VMEM((groups, 8, width), F32)]
        + [slots] * 6
        + [pltpu.SemaphoreType.DMA((2, 1))]
        + [pltpu.SemaphoreType.DMA((2, groups))] * 4,
        compiler_params=pltpu.CompilerParams(
            collective_id=0, has_side_effects=True, vmem_limit_bytes=limit
        ),
        name="layer_gradients",
    )(
        b_rows, c_rows, x_rows, grad_rows, cols,
        log_decay.T.reshape(groups, HEADS, length), span_rows,
    )
    row_sums = row_sums.reshape(heads, length)
    inside, x_in, g_in = (col_sums[:, i * heads : (i + 1) * heads] for i in range(3))
    both = span * jnp.sum(inner.reshape(heads, size), axis=1)
    position = jnp.arange(length)
    earlier = (position[:, None] > position[None, :]).astype(F32)
    change = g_in + row_sums.T - dt * inside
    d_log = (
        both[None, :]
        + jnp.dot(earlier, dt * x_in, precision=lax.Precision.HIGHEST)
        + jnp.dot((position[:, None] <= position[None, :]).astype(F32), change, precision=lax.Precision.HIGHEST)
    )
    d_dt = inside + x_in - decay_rate[None, :] * d_log
    grad_logit = d_dt * jax.nn.sigmoid(logit)
    grad_rate = -jnp.sum(dt * d_log, axis=0)
    members = lax.axis_size("dp")
    blocks = count * members
    piece = tokens.shape[1] // blocks
    chunks = max(1, min(4, piece // 8))
    rows = piece // chunks
    levels = blocks.bit_length() - 1
    rate_rows = jnp.pad(grad_rate.reshape(1, heads), ((0, 7), (0, 128 - heads)))
    weight_rows, rate_sum = pl.pallas_call(
        functools.partial(weight_kernel, count, members),
        in_specs=[vmem] * 3,
        out_specs=[vmem] * 2,
        out_shape=[
            jax.ShapeDtypeStruct((members * piece, 2 * state), F32),
            jax.ShapeDtypeStruct((8, 128), F32),
        ],
        scratch_shapes=[
            pltpu.VMEM((chunks, blocks, rows, 2 * state), F32),
            pltpu.VMEM((chunks, blocks, rows, 2 * state), F32),
            pltpu.VMEM((members, chunks, rows, 2 * state), F32),
            pltpu.VMEM((levels + 1, 8, 128), F32),
            pltpu.VMEM((levels, 8, 128), F32),
            pltpu.SemaphoreType.DMA((2, chunks, levels)),
            pltpu.SemaphoreType.DMA((2, chunks, members)),
            pltpu.SemaphoreType.DMA((2, levels)),
        ],
        compiler_params=pltpu.CompilerParams(
            collective_id=1, has_side_effects=True, vmem_limit_bytes=limit
        ),
        name="weight_gradient",
    )(tokens, grad_bc, rate_rows)
    rate_sum = rate_sum[0, :heads]
    return (grad_x[None], grad_logit[None], rate_sum, weight_rows)


def solution(mesh):
    placed = (
        P("dp", "seq", None),
        P(),
        P("dp", "seq", None),
        P("dp", "seq", None),
        P(),
        P("dp", "seq", None),
    )
    return jax.shard_map(
        shards,
        mesh=mesh,
        in_specs=placed,
        out_specs=(P("dp", "seq", None), P("dp", "seq", None), P(), P("seq", None)),
        check_vma=False,
    )
```

```python
import functools

import jax
import jax.numpy as jnp
from jax import lax
from jax.experimental import pallas as pl
from jax.experimental.pallas import tpu as pltpu
from jax.sharding import PartitionSpec as P

F32 = jnp.float32
BF16 = jnp.bfloat16
HEADS = 4


def dot(a, b, ca, cb):
    return lax.dot_general(a, b, (((ca,), (cb,)), ((), ())), preferred_element_type=F32)


def pair_columns(cols, j, size):
    rows = cols.shape[0]
    lane = lax.broadcasted_iota(jnp.int32, (rows, 2 * size), 1)
    return jnp.where(lane < size, cols[:, j : j + 1], cols[:, j + 1 : j + 2])


def layer_kernel(
    n, size, b_ref, c_ref, x_ref, g_ref, col_ref, row_ref, d_ref,
    dx_ref, rows_ref, cols_ref, ef_ref, gbc_ref,
    s_ref, a_ref, e_out, f_out, scores, d_scores, d_b, d_c,
    d_in, s_in, a_in, e_in, f_in, e_snd, f_snd,
    d_sem, s_sem, a_sem, e_sem, f_sem,
):
    chunks = s_ref.shape[0]
    length = b_ref.shape[0]
    state = b_ref.shape[1]
    width = 2 * size
    heads = chunks * HEADS
    nz = n // 2
    me = lax.axis_index("seq")
    odd = lax.rem(me, 2)
    z = lax.div(me, 2)
    partner = me + 1 - 2 * odd
    first, last = z == 0, z == nz - 1
    barrier = pltpu.get_barrier_semaphore()

    def greet(who):
        pl.semaphore_signal(
            barrier, inc=1, device_id={"seq": who}, device_id_type=pl.DeviceIdType.MESH
        )

    greet(partner)
    pl.when(jnp.logical_not(first))(lambda: greet(me - 2))
    pl.when(jnp.logical_not(last))(lambda: greet(me + 2))

    def send(src, dst, sems, k, who):
        return pltpu.make_async_remote_copy(
            src_ref=src, dst_ref=dst, send_sem=sems.at[0, k], recv_sem=sems.at[1, k],
            device_id={"seq": who}, device_id_type=pl.DeviceIdType.MESH,
        )

    def copy_d():
        return send(d_ref, d_in, d_sem, 0, partner)

    def copy_s(k):
        return send(s_ref.at[k], s_in.at[k], s_sem, k, partner)

    def copy_a(k):
        return send(a_ref.at[k], a_in.at[k], a_sem, k, partner)

    def copy_e(k):
        return send(e_snd.at[k], e_in.at[k], e_sem, k, me + 2)

    def copy_f(k):
        return send(f_snd.at[k], f_in.at[k], f_sem, k, me - 2)

    def pair_lanes(k, pair):
        return pl.ds(pl.multiple_of(k * (HEADS * size) + pair * width, width), width)

    def local(k, unused):
        cols = col_ref[k]
        for pair in range(HEADS // 2):
            lanes = pl.ds(pair * width, width)
            wide = pair_lanes(k, pair)
            j = 2 * pair
            to_end = pair_columns(cols, j + HEADS, size) * pair_columns(cols, j + 2 * HEADS, size)
            grow = pair_columns(cols, j + 3 * HEADS, size)
            xs = (x_ref[:, wide].astype(F32) * to_end).astype(BF16)
            gs = (g_ref[:, wide].astype(F32) * grow).astype(BF16)
            s_ref[k, :, lanes] = dot(b_ref[...], xs, 0, 0)
            a_ref[k, :, lanes] = dot(c_ref[...], gs, 0, 0)

        @pl.when(k > 0)
        def _():
            copy_s(k - 1).start()
            copy_a(k - 1).start()

        return unused

    end = jnp.logical_or(first, last)
    pl.when(end)(lambda: pl.semaphore_wait(barrier, min(nz, 2)))
    pl.when(jnp.logical_not(end))(lambda: pl.semaphore_wait(barrier, 3))
    copy_d().start()
    lax.fori_loop(0, chunks, local, 0)
    copy_s(chunks - 1).start()
    copy_a(chunks - 1).start()

    @pl.when(first)
    def _():
        e_in[...] = jnp.zeros_like(e_in)

    @pl.when(last)
    def _():
        f_in[...] = jnp.zeros_like(f_in)

    b, c = b_ref[...], c_ref[...]
    scores[...] = dot(b, c, 1, 1)
    d_scores[...] = jnp.zeros_like(d_scores)
    d_b[...] = jnp.zeros_like(d_b)
    d_c[...] = jnp.zeros_like(d_c)
    cols_ref[...] = jnp.zeros_like(cols_ref)
    copy_d().wait_recv()

    def advance(k, near, far, carry, out, snd, near_first):
        @pl.when(near_first)
        def _():
            value = carry[k]
            out[k] = value.astype(out.dtype)
            middle = d_ref[k, 0:1] * value + near[k]
            snd[k] = d_in[k, 0:1] * middle + far[k]

        @pl.when(jnp.logical_not(near_first))
        def _():
            middle = d_in[k, 0:1] * carry[k] + far[k]
            out[k] = middle.astype(out.dtype)
            snd[k] = d_ref[k, 0:1] * middle + near[k]

    def gradients(k):
        cols = col_ref[k]
        rows = row_ref[k]
        k_st = scores[...]
        causal = lax.broadcasted_iota(jnp.int32, (length, length), 1) >= lax.broadcasted_iota(
            jnp.int32, (length, length), 0
        )
        low = lax.broadcasted_iota(jnp.int32, (length, width), 1) < size
        place = lax.broadcasted_iota(jnp.int32, cols_ref.shape, 1) - k * HEADS
        result = cols_ref[...]
        q_sum = d_scores[...]
        b_sum, c_sum = d_b[...], d_c[...]
        for pair in range(HEADS // 2):
            lanes = pl.ds(pair * width, width)
            wide = pair_lanes(k, pair)
            x2, g2 = x_ref[:, wide], g_ref[:, wide]
            x2f, g2f = x2.astype(F32), g2.astype(F32)
            e2, f2 = e_out[k, :, lanes], f_out[k, :, lanes]
            j = 2 * pair
            dt2 = pair_columns(cols, j + HEADS, size)
            end2 = pair_columns(cols, j + 2 * HEADS, size)
            grow2 = pair_columns(cols, j + 3 * HEADS, size)
            g_low = jnp.where(low, g2, jnp.zeros_like(g2))
            g_high = jnp.where(low, jnp.zeros_like(g2), g2)
            g_both = jnp.concatenate([g_low, g_high], axis=0)
            gram = dot(x2, g_both, 1, 1)
            weights = []
            for side in range(2):
                h = j + side
                gap = rows[h : h + 1, :] - cols[:, h : h + 1]
                decay = jnp.exp(jnp.where(causal, gap, -jnp.inf))
                mg = decay * gram[:, side * length : (side + 1) * length]
                dt = cols[:, h + HEADS : h + HEADS + 1]
                q_sum = q_sum + mg * dt
                raw = mg * k_st
                rows_ref[k, h : h + 1, :] = jnp.sum(raw * dt, axis=0, keepdims=True)
                result = jnp.where(place == h, jnp.sum(raw, axis=1, keepdims=True), result)
                weights.append((decay * k_st).astype(BF16))
            z2 = dot(jnp.concatenate(weights, axis=1), g_both, 1, 0)
            z_in = dot(b, f2, 1, 0) * end2
            dx_ref[:, wide] = (dt2 * (z2 + z_in)).astype(dx_ref.dtype)
            y_in = dot(c, e2, 1, 0) * grow2
            xz, gy = x2f * z_in, g2f * y_in
            zero = jnp.zeros_like(xz)
            for side in range(2):
                h = j + side
                mask = low if side == 0 else jnp.logical_not(low)
                xs = jnp.sum(jnp.where(mask, xz, zero), axis=1, keepdims=True)
                gs = jnp.sum(jnp.where(mask, gy, zero), axis=1, keepdims=True)
                result = jnp.where(place == h + heads, xs, result)
                result = jnp.where(place == h + 2 * heads, gs, result)
            ef_ref[k, :, lanes] = jnp.sum(
                e2.astype(F32) * f2.astype(F32), axis=0, keepdims=True
            )
            b_sum = b_sum + dot((x2f * (end2 * dt2)).astype(BF16), f2, 1, 1)
            c_sum = c_sum + dot((g2f * grow2).astype(BF16), e2, 1, 1)
        cols_ref[...] = result
        d_scores[...] = q_sum
        d_b[...] = b_sum
        d_c[...] = c_sum

    def step(t, unused):
        kf = t - z

        @pl.when(jnp.logical_and(kf >= 0, kf < chunks))
        def _():
            copy_s(kf).wait_recv()
            pl.when(jnp.logical_not(first))(lambda: copy_e(kf).wait_recv())
            advance(kf, s_ref, s_in, e_in, e_out, e_snd, odd == 0)
            pl.when(jnp.logical_not(last))(lambda: copy_e(kf).start())

        kb = t - (nz - 1 - z)

        @pl.when(jnp.logical_and(kb >= 0, kb < chunks))
        def _():
            copy_a(kb).wait_recv()
            pl.when(jnp.logical_not(last))(lambda: copy_f(kb).wait_recv())
            advance(kb, a_ref, a_in, f_in, f_out, f_snd, odd == 1)
            pl.when(jnp.logical_not(first))(lambda: copy_f(kb).start())

        pl.when(t >= nz - 1)(lambda: gradients(t - (nz - 1)))
        return unused

    lax.fori_loop(0, chunks + nz - 1, step, 0)
    dk = d_scores[...].astype(BF16)
    gbc_ref[:, :state] = (d_b[...] + dot(dk, c, 1, 0)).astype(gbc_ref.dtype)
    gbc_ref[:, state:] = (d_c[...] + dot(dk, b, 0, 0)).astype(gbc_ref.dtype)
    copy_d().wait_send()

    def settle(k, unused):
        copy_s(k).wait_send()
        copy_a(k).wait_send()
        pl.when(jnp.logical_not(last))(lambda: copy_e(k).wait_send())
        pl.when(jnp.logical_not(first))(lambda: copy_f(k).wait_send())
        return unused

    lax.fori_loop(0, chunks, settle, 0)


def weight_kernel(
    n, m, t_ref, g_ref, rate_ref, out_ref, rate_out,
    acc, got, ring, r_acc, r_got, sem, out_sem, r_sem,
):
    chunks, blocks, rows = acc.shape[0], acc.shape[1], acc.shape[2]
    piece = chunks * rows
    seq, dp = lax.axis_index("seq"), lax.axis_index("dp")
    dp_steps, seq_steps, bit = [], [], 1
    while bit < m:
        dp_steps.append(("dp", bit, lax.rem(lax.div(dp, bit), 2)))
        bit *= 2
    bit = 1
    while bit < n:
        seq_steps.append(("seq", bit, lax.rem(lax.div(seq, bit), 2)))
        bit *= 2
    count = len(dp_steps) + len(seq_steps)
    orders = (dp_steps + seq_steps, dp_steps[:1] + seq_steps + dp_steps[1:])

    def peer(c, s):
        axis, bit, mine = orders[c % 2][s]
        return {axis: lax.axis_index(axis) + bit - 2 * bit * mine}

    def dp_peer(k):
        other, bit = dp, 1
        while bit < m:
            if k & bit:
                other = other + bit - 2 * bit * lax.rem(lax.div(dp, bit), 2)
            bit *= 2
        return {"dp": other}

    barrier = pltpu.get_barrier_semaphore()
    friends = [dp_peer(k) for k in range(1, m)] + [
        peer(0, s) for s in range(len(dp_steps), count)
    ]
    for friend in friends:
        pl.semaphore_signal(
            barrier, inc=1, device_id=friend, device_id_type=pl.DeviceIdType.MESH
        )

    starts, offsets = [], []
    for order in orders:
        base, width, total = 0, blocks, 0
        starts.append([])
        for unused, unused, mine in order:
            width //= 2
            starts[-1].append((base + width * mine, base + width * (1 - mine), width))
            base = base + width * mine
            if len(starts) == 1:
                offsets.append(total)
                total += width

    def copy(c, s):
        keep, give, size = starts[c % 2][s]
        return pltpu.make_async_remote_copy(
            src_ref=acc.at[c, pl.ds(give, size)],
            dst_ref=got.at[c, pl.ds(offsets[s], size)],
            send_sem=sem.at[0, c, s], recv_sem=sem.at[1, c, s],
            device_id=peer(c, s), device_id_type=pl.DeviceIdType.MESH,
        )

    def rate_copy(s):
        return pltpu.make_async_remote_copy(
            src_ref=r_acc.at[s], dst_ref=r_got.at[s],
            send_sem=r_sem.at[0, s], recv_sem=r_sem.at[1, s],
            device_id=peer(0, s), device_id_type=pl.DeviceIdType.MESH,
        )

    def out_copy(c, k):
        return pltpu.make_async_remote_copy(
            src_ref=ring.at[0, c], dst_ref=ring.at[k, c],
            send_sem=out_sem.at[0, c, k], recv_sem=out_sem.at[1, c, k],
            device_id=dp_peer(k), device_id_type=pl.DeviceIdType.MESH,
        )

    g = g_ref[...]
    r_acc[0] = rate_ref[...]
    block = 128
    for first in range(0, t_ref.shape[1], block):
        product = dot(t_ref[:, first : first + block], g, 0, 0)
        for part in range(0, block, rows):
            row = first + part
            owner, inner = row // (m * piece), row % (m * piece)
            chunk, place = inner % piece // rows, 0
            for axis, bit, unused in orders[chunk % 2]:
                index = inner // piece if axis == "dp" else owner
                place = 2 * place + index // bit % 2
            acc[chunk, place] = product[part : part + rows]
    pl.semaphore_wait(barrier, len(friends))
    for c in range(chunks):
        copy(c, 0).start()
    rate_copy(0).start()
    for turn in range(chunks + count):
        for c in range(chunks):
            s = turn - c
            if not 0 <= s < count:
                continue
            copy(c, s).wait_recv()
            keep, give, size = starts[c % 2][s]
            value = acc[c, pl.ds(keep, size)] + got[c, pl.ds(offsets[s], size)]
            if s + 1 < count:
                acc[c, pl.ds(keep, size)] = value
                copy(c, s + 1).start()
            else:
                ring[0, c] = value[0]
                for k in range(1, m):
                    out_copy(c, k).start()
        if turn < count:
            rate_copy(turn).wait_recv()
            r_acc[turn + 1] = r_acc[turn] + r_got[turn]
            if turn + 1 < count:
                rate_copy(turn + 1).start()
    rate_out[...] = r_acc[count]
    for c in range(chunks):
        for k in range(m):
            if k > 0:
                out_copy(c, k).wait_recv()
            where = dp_peer(k)["dp"] if k > 0 else dp
            out_ref[pl.ds(where * piece + c * rows, rows)] = ring[k, c]
    for c in range(chunks):
        for s in range(count):
            copy(c, s).wait_send()
        for k in range(1, m):
            out_copy(c, k).wait_send()
    for s in range(count):
        rate_copy(s).wait_send()


def shards(layer_input, projection, ssm_input, step_logit, decay_rate, output_grad):
    tokens, x_rows, logit, grad_rows = layer_input[0], ssm_input[0], step_logit[0], output_grad[0]
    length, full = x_rows.shape
    heads = logit.shape[1]
    size = full // heads
    state = projection.shape[1] // 2
    groups = heads // HEADS
    width = HEADS * size
    count = lax.axis_size("seq")
    projected = jnp.dot(tokens, projection, preferred_element_type=F32).astype(BF16)
    b_rows, c_rows = projected[:, :state], projected[:, state:]
    dt = jax.nn.softplus(logit)
    log_decay = jnp.cumsum(-decay_rate[None, :] * dt, axis=0)
    to_end = jnp.exp(log_decay[-1][None, :] - log_decay)
    grow = jnp.exp(log_decay)
    span = grow[-1]

    def by_group(value):
        return value.reshape(length, groups, HEADS).transpose(1, 0, 2)

    cols = jnp.concatenate([by_group(v) for v in (log_decay, dt, to_end, grow)], axis=2)
    span_rows = jnp.broadcast_to(
        jnp.broadcast_to(span.reshape(groups, 1, HEADS, 1), (groups, 1, HEADS, size)).reshape(
            groups, 1, width
        ),
        (groups, 8, width),
    )
    limit = 60 * 2**20
    vmem = pl.BlockSpec(memory_space=pltpu.VMEM)
    slots = pltpu.VMEM((groups, state, width), F32)
    half = pltpu.VMEM((groups, state, width), BF16)
    square = pltpu.VMEM((length, length), F32)
    sums = pltpu.VMEM((length, state), F32)
    grad_x, row_sums, col_sums, inner, grad_bc = pl.pallas_call(
        functools.partial(layer_kernel, count, size),
        in_specs=[vmem] * 7,
        out_specs=[vmem] * 5,
        out_shape=[
            jax.ShapeDtypeStruct((length, full), BF16),
            jax.ShapeDtypeStruct((groups, HEADS, length), F32),
            jax.ShapeDtypeStruct((length, 3 * heads), F32),
            jax.ShapeDtypeStruct((groups, 1, width), F32),
            jax.ShapeDtypeStruct((length, 2 * state), BF16),
        ],
        scratch_shapes=[slots, slots, half, half, square, square, sums, sums]
        + [pltpu.VMEM((groups, 8, width), F32)]
        + [slots] * 6
        + [pltpu.SemaphoreType.DMA((2, 1))]
        + [pltpu.SemaphoreType.DMA((2, groups))] * 4,
        compiler_params=pltpu.CompilerParams(
            collective_id=0, has_side_effects=True, vmem_limit_bytes=limit
        ),
        name="layer_gradients",
    )(
        b_rows, c_rows, x_rows, grad_rows, cols,
        log_decay.T.reshape(groups, HEADS, length), span_rows,
    )
    row_sums = row_sums.reshape(heads, length)
    inside, x_in, g_in = (col_sums[:, i * heads : (i + 1) * heads] for i in range(3))
    both = span * jnp.sum(inner.reshape(heads, size), axis=1)
    position = jnp.arange(length)
    earlier = (position[:, None] > position[None, :]).astype(F32)
    change = g_in + row_sums.T - dt * inside
    d_log = (
        both[None, :]
        + jnp.dot(earlier, dt * x_in, precision=lax.Precision.HIGHEST)
        + jnp.dot((position[:, None] <= position[None, :]).astype(F32), change, precision=lax.Precision.HIGHEST)
    )
    d_dt = inside + x_in - decay_rate[None, :] * d_log
    grad_logit = d_dt * jax.nn.sigmoid(logit)
    grad_rate = -jnp.sum(dt * d_log, axis=0)
    members = lax.axis_size("dp")
    blocks = count * members
    piece = tokens.shape[1] // blocks
    chunks = max(1, min(8, piece // 8))
    rows = piece // chunks
    levels = blocks.bit_length() - 1
    rate_rows = jnp.pad(grad_rate.reshape(1, heads), ((0, 7), (0, 128 - heads)))
    weight_rows, rate_sum = pl.pallas_call(
        functools.partial(weight_kernel, count, members),
        in_specs=[vmem] * 3,
        out_specs=[vmem] * 2,
        out_shape=[
            jax.ShapeDtypeStruct((members * piece, 2 * state), F32),
            jax.ShapeDtypeStruct((8, 128), F32),
        ],
        scratch_shapes=[
            pltpu.VMEM((chunks, blocks, rows, 2 * state), F32),
            pltpu.VMEM((chunks, blocks, rows, 2 * state), F32),
            pltpu.VMEM((members, chunks, rows, 2 * state), F32),
            pltpu.VMEM((levels + 1, 8, 128), F32),
            pltpu.VMEM((levels, 8, 128), F32),
            pltpu.SemaphoreType.DMA((2, chunks, levels)),
            pltpu.SemaphoreType.DMA((2, chunks, members)),
            pltpu.SemaphoreType.DMA((2, levels)),
        ],
        compiler_params=pltpu.CompilerParams(
            collective_id=1, has_side_effects=True, vmem_limit_bytes=limit
        ),
        name="weight_gradient",
    )(tokens, grad_bc, rate_rows)
    rate_sum = rate_sum[0, :heads]
    return (grad_x[None], grad_logit[None], rate_sum, weight_rows)


def solution(mesh):
    placed = (
        P("dp", "seq", None),
        P(),
        P("dp", "seq", None),
        P("dp", "seq", None),
        P(),
        P("dp", "seq", None),
    )
    return jax.shard_map(
        shards,
        mesh=mesh,
        in_specs=placed,
        out_specs=(P("dp", "seq", None), P("dp", "seq", None), P(), P("seq", None)),
        check_vma=False,
    )
```

```python
import functools

import jax
import jax.numpy as jnp
from jax import lax
from jax.experimental import pallas as pl
from jax.experimental.pallas import tpu as pltpu
from jax.sharding import PartitionSpec as P

F32 = jnp.float32
BF16 = jnp.bfloat16
HEADS = 4


def dot(a, b, ca, cb):
    return lax.dot_general(a, b, (((ca,), (cb,)), ((), ())), preferred_element_type=F32)


def pair_columns(cols, j, size):
    rows = cols.shape[0]
    lane = lax.broadcasted_iota(jnp.int32, (rows, 2 * size), 1)
    return jnp.where(lane < size, cols[:, j : j + 1], cols[:, j + 1 : j + 2])


def layer_kernel(
    n, size, b_ref, c_ref, x_ref, g_ref, col_ref, row_ref, d_ref,
    dx_ref, rows_ref, cols_ref, ef_ref, gbc_ref,
    s_ref, a_ref, e_out, f_out, scores, d_scores, d_b, d_c,
    d_in, s_in, a_in, e_in, f_in, e_snd, f_snd,
    d_sem, s_sem, a_sem, e_sem, f_sem,
):
    chunks = s_ref.shape[0]
    length = b_ref.shape[0]
    state = b_ref.shape[1]
    width = 2 * size
    heads = chunks * HEADS
    nz = n // 2
    me = lax.axis_index("seq")
    odd = lax.rem(me, 2)
    z = lax.div(me, 2)
    partner = me + 1 - 2 * odd
    first, last = z == 0, z == nz - 1
    barrier = pltpu.get_barrier_semaphore()

    def greet(who):
        pl.semaphore_signal(
            barrier, inc=1, device_id={"seq": who}, device_id_type=pl.DeviceIdType.MESH
        )

    greet(partner)
    pl.when(jnp.logical_not(first))(lambda: greet(me - 2))
    pl.when(jnp.logical_not(last))(lambda: greet(me + 2))

    def send(src, dst, sems, k, who):
        return pltpu.make_async_remote_copy(
            src_ref=src, dst_ref=dst, send_sem=sems.at[0, k], recv_sem=sems.at[1, k],
            device_id={"seq": who}, device_id_type=pl.DeviceIdType.MESH,
        )

    def copy_d():
        return send(d_ref, d_in, d_sem, 0, partner)

    def copy_s(k):
        return send(s_ref.at[k], s_in.at[k], s_sem, k, partner)

    def copy_a(k):
        return send(a_ref.at[k], a_in.at[k], a_sem, k, partner)

    def copy_e(k):
        return send(e_snd.at[k], e_in.at[k], e_sem, k, me + 2)

    def copy_f(k):
        return send(f_snd.at[k], f_in.at[k], f_sem, k, me - 2)

    def pair_lanes(k, pair):
        return pl.ds(pl.multiple_of(k * (HEADS * size) + pair * width, width), width)

    def local(k, unused):
        cols = col_ref[k]
        for pair in range(HEADS // 2):
            lanes = pl.ds(pair * width, width)
            wide = pair_lanes(k, pair)
            j = 2 * pair
            to_end = pair_columns(cols, j + HEADS, size) * pair_columns(cols, j + 2 * HEADS, size)
            grow = pair_columns(cols, j + 3 * HEADS, size)
            xs = (x_ref[:, wide].astype(F32) * to_end).astype(BF16)
            gs = (g_ref[:, wide].astype(F32) * grow).astype(BF16)
            s_ref[k, :, lanes] = dot(b_ref[...], xs, 0, 0)
            a_ref[k, :, lanes] = dot(c_ref[...], gs, 0, 0)

        @pl.when(k > 0)
        def _():
            copy_s(k - 1).start()
            copy_a(k - 1).start()

        return unused

    end = jnp.logical_or(first, last)
    pl.when(end)(lambda: pl.semaphore_wait(barrier, min(nz, 2)))
    pl.when(jnp.logical_not(end))(lambda: pl.semaphore_wait(barrier, 3))
    copy_d().start()
    lax.fori_loop(0, chunks, local, 0)
    copy_s(chunks - 1).start()
    copy_a(chunks - 1).start()

    @pl.when(first)
    def _():
        e_in[...] = jnp.zeros_like(e_in)

    @pl.when(last)
    def _():
        f_in[...] = jnp.zeros_like(f_in)

    b, c = b_ref[...], c_ref[...]
    scores[...] = dot(b, c, 1, 1)
    d_scores[...] = jnp.zeros_like(d_scores)
    d_b[...] = jnp.zeros_like(d_b)
    d_c[...] = jnp.zeros_like(d_c)
    cols_ref[...] = jnp.zeros_like(cols_ref)
    copy_d().wait_recv()

    def advance(k, near, far, carry, out, snd, near_first):
        @pl.when(near_first)
        def _():
            value = carry[k]
            out[k] = value.astype(out.dtype)
            middle = d_ref[k, 0:1] * value + near[k]
            snd[k] = d_in[k, 0:1] * middle + far[k]

        @pl.when(jnp.logical_not(near_first))
        def _():
            middle = d_in[k, 0:1] * carry[k] + far[k]
            out[k] = middle.astype(out.dtype)
            snd[k] = d_ref[k, 0:1] * middle + near[k]

    def gradients(k):
        cols = col_ref[k]
        rows = row_ref[k]
        k_st = scores[...]
        causal = lax.broadcasted_iota(jnp.int32, (length, length), 1) >= lax.broadcasted_iota(
            jnp.int32, (length, length), 0
        )
        low = lax.broadcasted_iota(jnp.int32, (length, width), 1) < size
        place = lax.broadcasted_iota(jnp.int32, cols_ref.shape, 1) - k * HEADS
        result = cols_ref[...]
        q_sum = d_scores[...]
        b_sum, c_sum = d_b[...], d_c[...]
        for pair in range(HEADS // 2):
            lanes = pl.ds(pair * width, width)
            wide = pair_lanes(k, pair)
            x2, g2 = x_ref[:, wide], g_ref[:, wide]
            x2f, g2f = x2.astype(F32), g2.astype(F32)
            e2, f2 = e_out[k, :, lanes], f_out[k, :, lanes]
            j = 2 * pair
            dt2 = pair_columns(cols, j + HEADS, size)
            end2 = pair_columns(cols, j + 2 * HEADS, size)
            grow2 = pair_columns(cols, j + 3 * HEADS, size)
            g_low = jnp.where(low, g2, jnp.zeros_like(g2))
            g_high = jnp.where(low, jnp.zeros_like(g2), g2)
            g_both = jnp.concatenate([g_low, g_high], axis=0)
            gram = dot(x2, g_both, 1, 1)
            weights = []
            for side in range(2):
                h = j + side
                gap = rows[h : h + 1, :] - cols[:, h : h + 1]
                decay = jnp.exp(jnp.where(causal, gap, -jnp.inf))
                mg = decay * gram[:, side * length : (side + 1) * length]
                dt = cols[:, h + HEADS : h + HEADS + 1]
                q_sum = q_sum + mg * dt
                raw = mg * k_st
                rows_ref[k, h : h + 1, :] = jnp.sum(raw * dt, axis=0, keepdims=True)
                result = jnp.where(place == h, jnp.sum(raw, axis=1, keepdims=True), result)
                weights.append((decay * k_st).astype(BF16))
            z2 = dot(jnp.concatenate(weights, axis=1), g_both, 1, 0)
            z_in = dot(b, f2, 1, 0) * end2
            dx_ref[:, wide] = (dt2 * (z2 + z_in)).astype(dx_ref.dtype)
            y_in = dot(c, e2, 1, 0) * grow2
            xz, gy = x2f * z_in, g2f * y_in
            zero = jnp.zeros_like(xz)
            for side in range(2):
                h = j + side
                mask = low if side == 0 else jnp.logical_not(low)
                xs = jnp.sum(jnp.where(mask, xz, zero), axis=1, keepdims=True)
                gs = jnp.sum(jnp.where(mask, gy, zero), axis=1, keepdims=True)
                result = jnp.where(place == h + heads, xs, result)
                result = jnp.where(place == h + 2 * heads, gs, result)
            ef_ref[k, :, lanes] = jnp.sum(
                e2.astype(F32) * f2.astype(F32), axis=0, keepdims=True
            )
            b_sum = b_sum + dot((x2f * (end2 * dt2)).astype(BF16), f2, 1, 1)
            c_sum = c_sum + dot((g2f * grow2).astype(BF16), e2, 1, 1)
        cols_ref[...] = result
        d_scores[...] = q_sum
        d_b[...] = b_sum
        d_c[...] = c_sum

    def step(t, unused):
        kf = t - z

        @pl.when(jnp.logical_and(kf >= 0, kf < chunks))
        def _():
            copy_s(kf).wait_recv()
            pl.when(jnp.logical_not(first))(lambda: copy_e(kf).wait_recv())
            advance(kf, s_ref, s_in, e_in, e_out, e_snd, odd == 0)
            pl.when(jnp.logical_not(last))(lambda: copy_e(kf).start())

        kb = t - (nz - 1 - z)

        @pl.when(jnp.logical_and(kb >= 0, kb < chunks))
        def _():
            copy_a(kb).wait_recv()
            pl.when(jnp.logical_not(last))(lambda: copy_f(kb).wait_recv())
            advance(kb, a_ref, a_in, f_in, f_out, f_snd, odd == 1)
            pl.when(jnp.logical_not(first))(lambda: copy_f(kb).start())

        pl.when(t >= nz - 1)(lambda: gradients(t - (nz - 1)))
        return unused

    lax.fori_loop(0, chunks + nz - 1, step, 0)
    dk = d_scores[...].astype(BF16)
    gbc_ref[:, :state] = (d_b[...] + dot(dk, c, 1, 0)).astype(gbc_ref.dtype)
    gbc_ref[:, state:] = (d_c[...] + dot(dk, b, 0, 0)).astype(gbc_ref.dtype)
    copy_d().wait_send()

    def settle(k, unused):
        copy_s(k).wait_send()
        copy_a(k).wait_send()
        pl.when(jnp.logical_not(last))(lambda: copy_e(k).wait_send())
        pl.when(jnp.logical_not(first))(lambda: copy_f(k).wait_send())
        return unused

    lax.fori_loop(0, chunks, settle, 0)


def weight_kernel(
    n, m, t_ref, g_ref, rate_ref, out_ref, rate_out,
    acc, got, ring, r_acc, r_got, sem, out_sem, r_sem,
):
    chunks, blocks, rows = acc.shape[0], acc.shape[1], acc.shape[2]
    piece = chunks * rows
    seq, dp = lax.axis_index("seq"), lax.axis_index("dp")
    dp_steps, seq_steps, bit = [], [], 1
    while bit < m:
        dp_steps.append(("dp", bit, lax.rem(lax.div(dp, bit), 2)))
        bit *= 2
    bit = 1
    while bit < n:
        seq_steps.append(("seq", bit, lax.rem(lax.div(seq, bit), 2)))
        bit *= 2
    count = len(dp_steps) + len(seq_steps)
    orders = (dp_steps + seq_steps, dp_steps[:1] + seq_steps + dp_steps[1:])

    def peer(c, s):
        axis, bit, mine = orders[c % 2][s]
        return {axis: lax.axis_index(axis) + bit - 2 * bit * mine}

    def dp_peer(k):
        other, bit = dp, 1
        while bit < m:
            if k & bit:
                other = other + bit - 2 * bit * lax.rem(lax.div(dp, bit), 2)
            bit *= 2
        return {"dp": other}

    barrier = pltpu.get_barrier_semaphore()
    friends = [dp_peer(k) for k in range(1, m)] + [
        peer(0, s) for s in range(len(dp_steps), count)
    ]
    for friend in friends:
        pl.semaphore_signal(
            barrier, inc=1, device_id=friend, device_id_type=pl.DeviceIdType.MESH
        )

    starts, offsets = [], []
    for order in orders:
        base, width, total = 0, blocks, 0
        starts.append([])
        for unused, unused, mine in order:
            width //= 2
            starts[-1].append((base + width * mine, base + width * (1 - mine), width))
            base = base + width * mine
            if len(starts) == 1:
                offsets.append(total)
                total += width

    def copy(c, s):
        keep, give, size = starts[c % 2][s]
        return pltpu.make_async_remote_copy(
            src_ref=acc.at[c, pl.ds(give, size)],
            dst_ref=got.at[c, pl.ds(offsets[s], size)],
            send_sem=sem.at[0, c, s], recv_sem=sem.at[1, c, s],
            device_id=peer(c, s), device_id_type=pl.DeviceIdType.MESH,
        )

    def rate_copy(s):
        return pltpu.make_async_remote_copy(
            src_ref=r_acc.at[s], dst_ref=r_got.at[s],
            send_sem=r_sem.at[0, s], recv_sem=r_sem.at[1, s],
            device_id=peer(0, s), device_id_type=pl.DeviceIdType.MESH,
        )

    def out_copy(c, k):
        return pltpu.make_async_remote_copy(
            src_ref=ring.at[0, c], dst_ref=ring.at[k, c],
            send_sem=out_sem.at[0, c, k], recv_sem=out_sem.at[1, c, k],
            device_id=dp_peer(k), device_id_type=pl.DeviceIdType.MESH,
        )

    g = g_ref[...]
    r_acc[0] = rate_ref[...]
    block = 128
    for first in range(0, t_ref.shape[1], block):
        product = dot(t_ref[:, first : first + block], g, 0, 0)
        for part in range(0, block, rows):
            row = first + part
            owner, inner = row // (m * piece), row % (m * piece)
            chunk, place = inner % piece // rows, 0
            for axis, bit, unused in orders[chunk % 2]:
                index = inner // piece if axis == "dp" else owner
                place = 2 * place + index // bit % 2
            acc[chunk, place] = product[part : part + rows]
    pl.semaphore_wait(barrier, len(friends))
    for c in range(chunks):
        copy(c, 0).start()
    rate_copy(0).start()
    for s in range(count):
        for c in range(chunks):
            copy(c, s).wait_recv()
            keep, give, size = starts[c % 2][s]
            value = acc[c, pl.ds(keep, size)] + got[c, pl.ds(offsets[s], size)]
            if s + 1 < count:
                acc[c, pl.ds(keep, size)] = value
                copy(c, s + 1).start()
            else:
                ring[0, c] = value[0]
                for k in range(1, m):
                    out_copy(c, k).start()
        rate_copy(s).wait_recv()
        r_acc[s + 1] = r_acc[s] + r_got[s]
        if s + 1 < count:
            rate_copy(s + 1).start()
    rate_out[...] = r_acc[count]
    for c in range(chunks):
        for k in range(m):
            if k > 0:
                out_copy(c, k).wait_recv()
            where = dp_peer(k)["dp"] if k > 0 else dp
            out_ref[pl.ds(where * piece + c * rows, rows)] = ring[k, c]
    for c in range(chunks):
        for s in range(count):
            copy(c, s).wait_send()
        for k in range(1, m):
            out_copy(c, k).wait_send()
    for s in range(count):
        rate_copy(s).wait_send()


def shards(layer_input, projection, ssm_input, step_logit, decay_rate, output_grad):
    tokens, x_rows, logit, grad_rows = layer_input[0], ssm_input[0], step_logit[0], output_grad[0]
    length, full = x_rows.shape
    heads = logit.shape[1]
    size = full // heads
    state = projection.shape[1] // 2
    groups = heads // HEADS
    width = HEADS * size
    count = lax.axis_size("seq")
    projected = jnp.dot(tokens, projection, preferred_element_type=F32).astype(BF16)
    b_rows, c_rows = projected[:, :state], projected[:, state:]
    dt = jax.nn.softplus(logit)
    log_decay = jnp.cumsum(-decay_rate[None, :] * dt, axis=0)
    to_end = jnp.exp(log_decay[-1][None, :] - log_decay)
    grow = jnp.exp(log_decay)
    span = grow[-1]

    def by_group(value):
        return value.reshape(length, groups, HEADS).transpose(1, 0, 2)

    cols = jnp.concatenate([by_group(v) for v in (log_decay, dt, to_end, grow)], axis=2)
    span_rows = jnp.broadcast_to(
        jnp.broadcast_to(span.reshape(groups, 1, HEADS, 1), (groups, 1, HEADS, size)).reshape(
            groups, 1, width
        ),
        (groups, 8, width),
    )
    limit = 60 * 2**20
    vmem = pl.BlockSpec(memory_space=pltpu.VMEM)
    slots = pltpu.VMEM((groups, state, width), F32)
    half = pltpu.VMEM((groups, state, width), BF16)
    square = pltpu.VMEM((length, length), F32)
    sums = pltpu.VMEM((length, state), F32)
    grad_x, row_sums, col_sums, inner, grad_bc = pl.pallas_call(
        functools.partial(layer_kernel, count, size),
        in_specs=[vmem] * 7,
        out_specs=[vmem] * 5,
        out_shape=[
            jax.ShapeDtypeStruct((length, full), BF16),
            jax.ShapeDtypeStruct((groups, HEADS, length), F32),
            jax.ShapeDtypeStruct((length, 3 * heads), F32),
            jax.ShapeDtypeStruct((groups, 1, width), F32),
            jax.ShapeDtypeStruct((length, 2 * state), BF16),
        ],
        scratch_shapes=[slots, slots, half, half, square, square, sums, sums]
        + [pltpu.VMEM((groups, 8, width), F32)]
        + [slots] * 6
        + [pltpu.SemaphoreType.DMA((2, 1))]
        + [pltpu.SemaphoreType.DMA((2, groups))] * 4,
        compiler_params=pltpu.CompilerParams(
            collective_id=0, has_side_effects=True, vmem_limit_bytes=limit
        ),
        name="layer_gradients",
    )(
        b_rows, c_rows, x_rows, grad_rows, cols,
        log_decay.T.reshape(groups, HEADS, length), span_rows,
    )
    row_sums = row_sums.reshape(heads, length)
    inside, x_in, g_in = (col_sums[:, i * heads : (i + 1) * heads] for i in range(3))
    both = span * jnp.sum(inner.reshape(heads, size), axis=1)
    position = jnp.arange(length)
    earlier = (position[:, None] > position[None, :]).astype(F32)
    change = g_in + row_sums.T - dt * inside
    d_log = (
        both[None, :]
        + jnp.dot(earlier, dt * x_in, precision=lax.Precision.HIGHEST)
        + jnp.dot((position[:, None] <= position[None, :]).astype(F32), change, precision=lax.Precision.HIGHEST)
    )
    d_dt = inside + x_in - decay_rate[None, :] * d_log
    grad_logit = d_dt * jax.nn.sigmoid(logit)
    grad_rate = -jnp.sum(dt * d_log, axis=0)
    members = lax.axis_size("dp")
    blocks = count * members
    piece = tokens.shape[1] // blocks
    chunks = max(1, min(4, piece // 8))
    rows = piece // chunks
    levels = blocks.bit_length() - 1
    rate_rows = jnp.pad(grad_rate.reshape(1, heads), ((0, 7), (0, 128 - heads)))
    weight_rows, rate_sum = pl.pallas_call(
        functools.partial(weight_kernel, count, members),
        in_specs=[vmem] * 3,
        out_specs=[vmem] * 2,
        out_shape=[
            jax.ShapeDtypeStruct((members * piece, 2 * state), F32),
            jax.ShapeDtypeStruct((8, 128), F32),
        ],
        scratch_shapes=[
            pltpu.VMEM((chunks, blocks, rows, 2 * state), F32),
            pltpu.VMEM((chunks, blocks, rows, 2 * state), F32),
            pltpu.VMEM((members, chunks, rows, 2 * state), F32),
            pltpu.VMEM((levels + 1, 8, 128), F32),
            pltpu.VMEM((levels, 8, 128), F32),
            pltpu.SemaphoreType.DMA((2, chunks, levels)),
            pltpu.SemaphoreType.DMA((2, chunks, members)),
            pltpu.SemaphoreType.DMA((2, levels)),
        ],
        compiler_params=pltpu.CompilerParams(
            collective_id=1, has_side_effects=True, vmem_limit_bytes=limit
        ),
        name="weight_gradient",
    )(tokens, grad_bc, rate_rows)
    rate_sum = rate_sum[0, :heads]
    return (grad_x[None], grad_logit[None], rate_sum, weight_rows)


def solution(mesh):
    placed = (
        P("dp", "seq", None),
        P(),
        P("dp", "seq", None),
        P("dp", "seq", None),
        P(),
        P("dp", "seq", None),
    )
    return jax.shard_map(
        shards,
        mesh=mesh,
        in_specs=placed,
        out_specs=(P("dp", "seq", None), P("dp", "seq", None), P(), P("seq", None)),
        check_vma=False,
    )
```
